32 devices in a mesh: lev: 4 (over y, x), lat: 8 (over z, core).
Axes of the slice: x: 2, y: 2, z: 4, core: 2. Of those that a mesh axis runs over, the one named last changes fastest.
Arguments:
- zonal_velocity: bfloat16 [8, 1280, 2560], P(None, 'lat', 'lev'), may hold values from -6 to 6
- meridional_velocity: bfloat16 [8, 1280, 2560], P(None, 'lat', 'lev'), may hold values from -6 to 6
- air_warmth: bfloat16 [8, 1280, 2560], P(None, 'lat', 'lev'), may hold values from -6 to 6
- pressure_integration_operator: bfloat16 [8, 8], replicated, may hold values from -2 to 2
- quadrature_factors_north: float32 [640], replicated, may hold values from 0.3 to 1.7
- associated_polynomial_table: bfloat16 [320, 641, 640], P('lat'), may hold values from -0.15625 to 0.15625
- position_wavenumber_couples: int32 [320], replicated, may hold values from 0 to 319, each once
- layer_projection_operator: bfloat16 [8, 8], replicated, may hold values from -2 to 2
- eigen_reconstruction_operator: bfloat16 [8, 8], replicated, may hold values from -2 to 2
- eigen_backward_factors: float32 [8], replicated, may hold values from 0.1 to 10
Outputs:
- tendency_fourier: float32 [2, 8, 320, 2, 2, 1280], P(None, 'lev', 'lat')
The draws below stay inside these ranges and needn't reach their ends.
Inputs may be any that keep to these rules, and one draw needn't show every extreme that they name: `position_wavenumber_couples`: every slot number from 0 to 319 names a different pair.
All inputs are finite; a program needn't handle non-finite values.
Results may differ from the reference program's by a relative error of at most 0.0072.
Values may be sent and summed in bfloat16 or wider, within the bound.
No kernel may reach another device: no remote copies, remote signals or barrier semaphores. Data moves between devices by JAX's collectives and lax.ppermute only.
A program may use at most 128 MiB of HBM per device.

```python
import math
import jax
import jax.numpy as jnp
from jax import lax

MERIDIAN_TOTAL = 2560
PARALLEL_TOTAL = 1280
M = 640
VARS = 2
LAYER_TOTAL = 8
NPAIR = 320
N_LAT = 8


def block_scale(rng, extent, shards, smallest, largest):
    level, own = 1.0, jax.random.fold_in(rng, 6)
    for dim, blocks in shards:
        draws = jnp.exp(jax.random.uniform(jax.random.fold_in(own, dim), (blocks,), jnp.float32, smallest / len(shards), largest / len(shards)))
        level = level * jnp.repeat(draws, extent[dim] // blocks).reshape([-1 if axis == dim else 1 for axis in range(len(extent))])
    return level


def gaussian(own_key, dims, deviation, most, cuts=(), kind=jnp.bfloat16):
    level = block_scale(own_key, dims, cuts, -0.22, 0.18) if cuts else 1.0
    values = jax.random.normal(own_key, dims, jnp.float32) * deviation * level
    return jnp.minimum(jnp.maximum(values, -most), most).astype(kind)


def setup_inputs(seed: int = 0) -> dict:
    seeds = jax.random.split(jax.random.key(seed), 11)
    zonal_velocity = gaussian(seeds[0], (LAYER_TOTAL, PARALLEL_TOTAL, MERIDIAN_TOTAL), 1.0, 6.0, ((1, 8), (2, 4)))
    meridional_velocity = gaussian(seeds[1], (LAYER_TOTAL, PARALLEL_TOTAL, MERIDIAN_TOTAL), 1.0, 6.0, ((1, 8), (2, 4)))
    air_warmth = gaussian(seeds[2], (LAYER_TOTAL, PARALLEL_TOTAL, MERIDIAN_TOTAL), 1.0, 6.0, ((1, 8), (2, 4)))
    pressure_integration_operator = gaussian(seeds[3], (LAYER_TOTAL, LAYER_TOTAL), LAYER_TOTAL ** -0.5, 2.0)
    quadrature_factors_north = jnp.clip(jax.random.uniform(seeds[4], (PARALLEL_TOTAL // 2,), jnp.float32, 0.3, 1.7), 0.3, 1.7)
    associated_polynomial_table = gaussian(seeds[5], (NPAIR, M + 1, PARALLEL_TOTAL // 2), PARALLEL_TOTAL ** -0.5, 0.15625, ((0, 8),))
    position_wavenumber_couples = jax.random.permutation(seeds[6], NPAIR).astype(jnp.int32)
    layer_projection_operator = gaussian(seeds[7], (LAYER_TOTAL, LAYER_TOTAL), LAYER_TOTAL ** -0.5, 2.0)
    eigen_reconstruction_operator = gaussian(seeds[8], (LAYER_TOTAL, LAYER_TOTAL), LAYER_TOTAL ** -0.5, 2.0)
    eigen_backward_factors = jnp.clip(jnp.exp(jax.random.uniform(seeds[9], (LAYER_TOTAL,), jnp.float32, math.log(0.1), math.log(10.0))), 0.1, 10.0)
    return dict(zonal_velocity=zonal_velocity, meridional_velocity=meridional_velocity, air_warmth=air_warmth, pressure_integration_operator=pressure_integration_operator, quadrature_factors_north=quadrature_factors_north, associated_polynomial_table=associated_polynomial_table, position_wavenumber_couples=position_wavenumber_couples, layer_projection_operator=layer_projection_operator, eigen_reconstruction_operator=eigen_reconstruction_operator, eigen_backward_factors=eigen_backward_factors)


def fourier_table(position_wavenumber_couples, lon_count, wave_count):
    repeated = jnp.repeat(position_wavenumber_couples, 4)
    column = jnp.arange(repeated.shape[0], dtype=jnp.int32)
    wavenumber = jnp.where(column // 2 % 2 == 0, repeated, wave_count - 1 - repeated)
    longitude = jnp.arange(lon_count, dtype=jnp.int32)
    phase_index = longitude[:, None] * wavenumber[None, :] % lon_count
    radians = phase_index.astype(jnp.float32) * (2.0 * math.pi / lon_count)
    values = jnp.where(column % 2 == 0, jnp.cos(radians), -jnp.sin(radians)) / math.sqrt(lon_count)
    return values.astype(jnp.bfloat16)

def row_layout(low_waves, wave_count, row_index):
    row_grid = row_index[None, :]
    low_grid = low_waves[:, None]
    boundary = wave_count - low_grid
    second_part = row_grid >= boundary
    parity = jnp.where(second_part, row_grid - boundary, row_grid) % 2
    degree = jnp.where(second_part, row_grid - 1, low_grid + row_grid)
    return (second_part, parity, degree)

def row_selector(second_part, parity):
    choices_two = jnp.arange(2, dtype=jnp.int32)
    parity_hit = parity[..., None] == choices_two
    part_hit = second_part.astype(jnp.int32)[..., None] == choices_two
    return parity_hit[..., :, None] & part_hit[..., None, :]

def damping(degree, eigen_backward_factors, wave_count):
    total = degree.astype(jnp.float32)
    factor = total * (total + 1.0) / float(wave_count * wave_count)
    return 1.0 / (1.0 + factor[:, :, None] * eigen_backward_factors[None, None, :])

def forward_legendre(by_wave, associated_polynomial_table, quadrature_factors_north, own_pairs, wave_count):
    field_count, layer_tally, lat_count, column_count = by_wave.shape
    half_rows = lat_count // 2
    slot_count = column_count // 4
    northern = by_wave[:, :, :half_rows].astype(jnp.float32)
    southern = by_wave[:, :, half_rows:][:, :, ::-1].astype(jnp.float32)
    folded = jnp.stack([northern + southern, northern - southern]) * quadrature_factors_north[:, None]
    folded = folded.astype(jnp.bfloat16).reshape(2, field_count, layer_tally, half_rows, slot_count, 2, 2)
    folded = jnp.transpose(folded, (4, 3, 0, 5, 6, 1, 2)).reshape(slot_count, half_rows, -1)
    product = jnp.einsum('srl,slc->src', associated_polynomial_table.astype(jnp.float32), folded.astype(jnp.float32))
    product = product.reshape(slot_count, wave_count + 1, 2, 2, 2, field_count, layer_tally)
    layout = row_layout(own_pairs, wave_count, jnp.arange(wave_count + 1, dtype=jnp.int32))
    chosen = row_selector(layout[0], layout[1])
    return lax.optimization_barrier(jnp.sum(jnp.where(chosen[..., None, None, None], product, 0.0), axis=(2, 3))).astype(jnp.bfloat16)

def inverse_legendre(implicit, associated_polynomial_table, own_pairs, wave_count):
    slot_count = implicit.shape[0]
    row_total = implicit.shape[1]
    field_count = implicit.shape[3]
    layer_tally = implicit.shape[4]
    layout = row_layout(own_pairs, wave_count, jnp.arange(row_total, dtype=jnp.int32))
    chosen = row_selector(layout[0], layout[1])
    spread = jnp.where(chosen[..., None, None, None], implicit[:, :, None, None], jnp.zeros((), implicit.dtype))
    spread = spread.reshape(slot_count, row_total, -1)
    summed = jnp.einsum('srl,src->slc', associated_polynomial_table.astype(jnp.float32), spread.astype(jnp.float32))
    summed = summed.reshape(slot_count, associated_polynomial_table.shape[2], 2, 2, 2, field_count, layer_tally)
    northern = summed[:, :, 0] + summed[:, :, 1]
    southern = (summed[:, :, 0] - summed[:, :, 1])[:, ::-1]
    latitudes = jnp.concatenate([northern, southern], axis=1)
    return jnp.transpose(latitudes, (4, 5, 0, 2, 3, 1))

def reference(zonal_velocity, meridional_velocity, air_warmth, pressure_integration_operator, quadrature_factors_north, associated_polynomial_table, position_wavenumber_couples, layer_projection_operator, eigen_reconstruction_operator, eigen_backward_factors):
    transform = fourier_table(position_wavenumber_couples, MERIDIAN_TOTAL, M)
    air_warmth_unrolled = air_warmth.reshape(LAYER_TOTAL, -1)

    def lone_layer(level_inputs):
        eastward, northward, warmth_spectrum_field, pressure_integration_line = level_inputs
        gravity_potential_surface = jnp.dot(pressure_integration_line, air_warmth_unrolled, preferred_element_type=jnp.float32).reshape(PARALLEL_TOTAL, MERIDIAN_TOTAL)
        eastward = eastward.astype(jnp.float32)
        northward = northward.astype(jnp.float32)
        warmth_spectrum_field = warmth_spectrum_field.astype(jnp.float32)
        products = jnp.stack([eastward * northward + gravity_potential_surface, (eastward + northward) * warmth_spectrum_field]).astype(jnp.bfloat16)
        harmonic_coefficients_field = jnp.dot(products.reshape(-1, MERIDIAN_TOTAL), transform, preferred_element_type=jnp.float32)
        return harmonic_coefficients_field.astype(jnp.bfloat16).reshape(VARS, PARALLEL_TOTAL, -1)
    harmonic_coefficients_field = lax.map(lone_layer, (zonal_velocity, meridional_velocity, air_warmth, pressure_integration_operator))
    harmonic_coefficients_field = jnp.transpose(harmonic_coefficients_field, (1, 0, 2, 3))
    slot_block = NPAIR // N_LAT
    fourier_blocks = jnp.moveaxis(harmonic_coefficients_field.reshape(VARS, LAYER_TOTAL, PARALLEL_TOTAL, N_LAT, slot_block * 4), 3, 0)
    legendre_blocks = associated_polynomial_table.reshape(N_LAT, slot_block, M + 1, PARALLEL_TOTAL // 2)
    pair_blocks = position_wavenumber_couples.reshape(N_LAT, slot_block)

    def forward_block(block_inputs):
        return forward_legendre(block_inputs[0], block_inputs[1], quadrature_factors_north, block_inputs[2], M)
    spectral = lax.map(forward_block, (fourier_blocks, legendre_blocks, pair_blocks))
    spectral = spectral.reshape(NPAIR, M + 1, 2, VARS, LAYER_TOTAL)
    flat_rows = spectral.reshape(-1, LAYER_TOTAL)
    mode_values = jnp.dot(flat_rows, layer_projection_operator.T, preferred_element_type=jnp.float32).reshape(spectral.shape)
    degree = row_layout(position_wavenumber_couples, M, jnp.arange(M + 1, dtype=jnp.int32))[2]
    damped = (mode_values * damping(degree, eigen_backward_factors, M)[:, :, None, None, :]).astype(jnp.bfloat16)
    implicit = jnp.dot(damped.reshape(-1, LAYER_TOTAL), eigen_reconstruction_operator.T, preferred_element_type=jnp.float32)
    implicit = implicit.reshape(spectral.shape).astype(jnp.bfloat16)
    implicit_blocks = implicit.reshape(N_LAT, slot_block, M + 1, 2, VARS, LAYER_TOTAL)

    def inverse_block(block_inputs):
        return inverse_legendre(block_inputs[0], block_inputs[1], block_inputs[2], M)
    result = lax.map(inverse_block, (implicit_blocks, legendre_blocks, pair_blocks))
    result = jnp.moveaxis(result, 0, 2)
    return result.reshape(VARS, LAYER_TOTAL, NPAIR, 2, 2, PARALLEL_TOTAL)
```

```python
import math

import jax
import jax.numpy as jnp
from jax import lax
from jax.experimental import pallas as pl
from jax.experimental.pallas import tpu as pltpu
from jax.sharding import PartitionSpec as P

BF = jnp.bfloat16
F32 = jnp.float32
LANE = 128
GROUP = 8
SUB = 32
CHUNKS = ((0, 2), (2, 5))


def products_call(u, v, t, operator, lev, first, count):
    levels, band, lons = u.shape
    own = levels // lev

    def body(op, u_ref, v_ref, t_ref, out):
        for tile in range(lons // LANE):
            at = slice(tile * LANE, (tile + 1) * LANE)
            warm = [t_ref[j, :, at].astype(F32) for j in range(levels)]
            for k in range(levels):
                height = op[k, 0] * warm[0]
                for j in range(1, levels):
                    height = height + op[k, j] * warm[j]
                east = u_ref[k, :, at].astype(F32)
                north = v_ref[k, :, at].astype(F32)
                out[k // own, 0, k % own, :, at] = (east * north + height).astype(BF)
                out[k // own, 0, own + k % own, :, at] = ((east + north) * warm[k]).astype(BF)

    grid_in = pl.BlockSpec((levels, SUB, lons), lambda h: (0, first + h, 0))
    return pl.pallas_call(
        body,
        name="products",
        grid=(count,),
        in_specs=[pl.BlockSpec(memory_space=pltpu.SMEM), grid_in, grid_in, grid_in],
        out_specs=pl.BlockSpec((lev, 1, 2 * own, SUB, lons), lambda h: (0, h, 0, 0, 0)),
        out_shape=jax.ShapeDtypeStruct((lev, count, 2 * own, SUB, lons), BF),
    )(operator.astype(F32), u, v, t)


def wave_rows_call(couples, lon_count, wave_count):
    rows = 4 * couples.shape[0]
    row = jnp.arange(rows, dtype=jnp.int32)
    low = jnp.repeat(couples, 4)
    wave = jnp.where(row // 2 % 2 == 0, low, wave_count - 1 - low)[:, None]
    lane = jnp.arange(LANE, dtype=jnp.int32)[None, :]
    unit = 2.0 * math.pi / lon_count
    start = (wave * lane % lon_count).astype(F32) * unit
    step = jnp.broadcast_to((wave * LANE % lon_count).astype(F32) * unit, (rows, LANE))
    scale = 1.0 / math.sqrt(lon_count)
    cosine, sine = jnp.cos(start) * scale, jnp.sin(start) * scale
    is_sine = (row % 2 == 1)[:, None]
    first = jnp.where(is_sine, -sine, cosine)
    second = jnp.where(is_sine, cosine, sine)
    block = GROUP * 4

    def body(a_ref, b_ref, c_ref, s_ref, out):
        a, b, c, s = a_ref[...], b_ref[...], c_ref[...], s_ref[...]
        for tile in range(lon_count // LANE):
            out[:, tile * LANE : (tile + 1) * LANE] = a.astype(BF)
            a, b = a * c - b * s, b * c + a * s

    spec = pl.BlockSpec((block, LANE), lambda i: (i, 0))
    return pl.pallas_call(
        body,
        name="wave_rows",
        grid=(rows // block,),
        in_specs=[spec] * 4,
        out_specs=pl.BlockSpec((block, lon_count), lambda i: (i, 0)),
        out_shape=jax.ShapeDtypeStruct((rows, lon_count), BF),
    )(first, second, jnp.cos(step), jnp.sin(step))


def fourier_call(waves, pieces, steps=4):
    parts, rows, lons = pieces.shape
    columns = waves.shape[0]
    block = columns // steps

    def body(w_ref, x_ref, out):
        total = None
        for j in range(parts):
            term = lax.dot_general(
                w_ref[:, j * lons : (j + 1) * lons],
                x_ref[j],
                (((1,), (1,)), ((), ())),
                preferred_element_type=F32,
            )
            total = term if total is None else total + term
        out[...] = total.astype(BF)

    return pl.pallas_call(
        body,
        name="fourier",
        grid=(steps,),
        in_specs=[
            pl.BlockSpec((block, parts * lons), lambda i: (i, 0)),
            pl.BlockSpec((parts, rows, lons), lambda i: (0, 0, 0)),
        ],
        out_specs=pl.BlockSpec((block, rows), lambda i: (i, 0)),
        out_shape=jax.ShapeDtypeStruct((columns, rows), BF),
    )(waves, pieces)


def by_slot(index, pairs, group):
    value = jnp.full(index.shape, pairs[group * GROUP], jnp.int32)
    for s in range(1, GROUP):
        value = jnp.where(index == s, pairs[group * GROUP + s], value)
    return value


def part_code(pairs, group, wave_count, half, par, lanes):
    lane = lax.broadcasted_iota(jnp.int32, (1, lanes), 1)
    slot = lane % GROUP
    r = 2 * (lane // GROUP + half) + par
    low = by_slot(slot, pairs, group)
    return 2 * slot + (r >= wave_count - low).astype(jnp.int32)


def forward_call(pairs, received, chunks, table, quadrature, lev):
    row_total, slots, half_lat = table.shape
    wave_count = row_total - 1
    bands = received[0].shape[0]
    units = chunks[-1][1]
    groups = slots // GROUP
    row_block = GROUP * 4
    fields = LANE // SUB
    rows = fields * row_block
    per = wave_count // 2 * GROUP
    piece = per * 2 // lev
    where_unit = {}
    for number, (lo, hi) in enumerate(chunks):
        for unit in range(lo, hi):
            where_unit[unit] = (number, unit - lo)

    def body(pairs_ref, *refs):
        recv = refs[: len(chunks)]
        table_ref, quad_ref, out, spread = refs[len(chunks) :]
        group = pl.program_id(0)
        lane = lax.broadcasted_iota(jnp.int32, (row_block, LANE), 1)
        within, place = lane % SUB, lane // SUB
        row = lax.broadcasted_iota(jnp.int32, (row_block, LANE), 0)
        low = by_slot(row // 4, pairs_ref, group)
        second = row // 2 % 2
        signs = [(1 - 2 * ((par + second * low) % 2)).astype(F32) for par in range(2)]

        def tile(band, unit):
            number, local = where_unit[unit]
            return recv[number][band, :, local * LANE : (local + 1) * LANE].astype(F32)

        for target in range(half_lat // LANE):
            at = slice(target * LANE, (target + 1) * LANE)
            north_tiles, south_tiles = [], []
            for d in range(fields):
                beta = fields * target + d
                band, unit = beta // units, beta % units
                north_tiles.append(tile(band, unit))
                south_tiles.append(tile(bands - 1 - band, units - 1 - unit))
            weight = quad_ref[0:1, at]
            for f in range(fields):
                north = jnp.zeros((row_block, LANE), F32)
                south = jnp.zeros((row_block, LANE), F32)
                for d in range(fields):
                    moved = jnp.take_along_axis(north_tiles[d], f * SUB + within, axis=1)
                    north = jnp.where(place == d, moved, north)
                    moved = jnp.take_along_axis(south_tiles[d], f * SUB + SUB - 1 - within, axis=1)
                    south = jnp.where(place == d, moved, south)
                for par in range(2):
                    folded = (north + signs[par] * south) * weight
                    spread[par, f * row_block : (f + 1) * row_block, at] = folded.astype(BF)
        to = lax.broadcasted_iota(jnp.int32, (rows, rows), 0)
        source = lax.broadcasted_iota(jnp.int32, (rows, rows), 1)
        wanted = to // 2 % fields * row_block + to // (2 * fields) * 2 + to % 2
        order = (source == wanted).astype(BF)
        whole = table_ref[0:wave_count].reshape(wave_count // 2, 2, GROUP, half_lat)
        last = table_ref[wave_count]
        out[...] = jnp.zeros(out.shape, BF)
        for par in range(2):
            field = jnp.dot(order, spread[par], preferred_element_type=F32).astype(BF)
            matrix = whole[:, par].reshape(per, half_lat)
            product = lax.dot_general(
                field, matrix, (((1,), (1,)), ((), ())), preferred_element_type=F32
            )
            code = part_code(pairs_ref, group, wave_count, 0, par, per)
            kept = jnp.zeros((GROUP, per), F32)
            for b in range(2 * GROUP):
                kept = kept + jnp.where(code == b, product[b * 8 : (b + 1) * 8], 0.0)
            kept = kept.astype(BF)
            for h in range(lev // 2):
                out[par * (lev // 2) + h, 0, :, 0:piece] = kept[:, h * piece : (h + 1) * piece]
            if par == 0:
                ending = lax.dot_general(
                    field, last, (((1,), (1,)), ((), ())), preferred_element_type=F32
                )
                lane8 = lax.broadcasted_iota(jnp.int32, (1, GROUP), 1)
                kept = jnp.zeros((GROUP, GROUP), F32)
                for b in range(GROUP):
                    kept = kept + jnp.where(lane8 == b, ending[b * 16 + 8 : b * 16 + 16], 0.0)
                out[lev // 2 - 1, 0, :, piece : piece + GROUP] = kept.astype(BF)

    recv_specs = [
        pl.BlockSpec((bands, row_block, (hi - lo) * LANE), lambda g, *_: (0, g, 0))
        for lo, hi in chunks
    ]
    return pl.pallas_call(
        body,
        name="forward",
        grid_spec=pltpu.PrefetchScalarGridSpec(
            num_scalar_prefetch=1,
            grid=(groups,),
            in_specs=recv_specs
            + [
                pl.BlockSpec((row_total, GROUP, half_lat), lambda g, *_: (0, g, 0)),
                pl.BlockSpec((1, half_lat), lambda g, *_: (0, 0)),
            ],
            out_specs=pl.BlockSpec((lev, 1, 8, piece + LANE), lambda g, *_: (0, g, 0, 0)),
            scratch_shapes=[pltpu.VMEM((2, rows, half_lat), BF)],
        ),
        out_shape=jax.ShapeDtypeStruct((lev, groups, 8, piece + LANE), BF),
    )(pairs, *received, table, quadrature[None, :])


def mix_matrix(operator, own):
    levels = operator.shape[0]
    n = levels * 4
    row = jnp.arange(n, dtype=jnp.int32)
    level = row // (4 * own) * own + row // 2 % own
    rest = row // (2 * own) % 2 * 2 + row % 2
    hot = (level[:, None] == jnp.arange(levels)[None, :]).astype(BF)
    spread = jnp.dot(jnp.dot(hot, operator, preferred_element_type=F32).astype(BF), hot.T,
                     preferred_element_type=F32)
    return jnp.where(rest[:, None] == rest[None, :], spread, 0.0).astype(BF), level


def implicit_call(pairs, position, received, project, rebuild, factors, wave_count):
    lev, groups, eight, lanes = received.shape
    n = lev * eight
    piece = lanes - LANE

    def body(pairs_ref, pos_ref, x_ref, p_ref, r_ref, f_ref, out):
        group = pl.program_id(0)
        place = pos_ref[0]
        par = place // (lev // 2)
        half = place % (lev // 2) * (piece // GROUP)
        lane = lax.broadcasted_iota(jnp.int32, (1, lanes), 1)
        r = 2 * (lane // GROUP + half) + par
        low = by_slot(lane % GROUP, pairs_ref, group)
        degree = jnp.where(r >= wave_count - low, r - 1, low + r).astype(F32)
        factor = degree * (degree + 1.0) / float(wave_count * wave_count)
        damping = 1.0 / (1.0 + factor * f_ref[:, 0:1])
        values = x_ref[...].reshape(n, lanes)
        modes = jnp.dot(p_ref[...], values, preferred_element_type=F32)
        damped = (modes * damping).astype(BF)
        result = jnp.dot(r_ref[...], damped, preferred_element_type=F32)
        out[...] = result.astype(BF).reshape(lev, 1, eight, lanes)

    block = pl.BlockSpec((lev, 1, eight, lanes), lambda g, *_: (0, g, 0, 0))
    small = pl.BlockSpec((n, n), lambda g, *_: (0, 0))
    return pl.pallas_call(
        body,
        name="implicit",
        grid_spec=pltpu.PrefetchScalarGridSpec(
            num_scalar_prefetch=2,
            grid=(groups,),
            in_specs=[block, small, small, pl.BlockSpec((n, LANE), lambda g, *_: (0, 0))],
            out_specs=block,
        ),
        out_shape=jax.ShapeDtypeStruct(received.shape, BF),
    )(pairs, position, received, project, rebuild, factors)


def inverse_call(pairs, implicit, table):
    row_total, slots, half_lat = table.shape
    wave_count = row_total - 1
    lev, groups, eight, lanes = implicit.shape
    piece = lanes - LANE
    per = wave_count // 2 * GROUP
    rows = 2 * GROUP * eight
    own = eight // 4

    def body(pairs_ref, x_ref, table_ref, out):
        group = pl.program_id(0)
        whole = table_ref[0:wave_count].reshape(wave_count // 2, 2, GROUP, half_lat)
        sums = []
        for par in range(2):
            value = jnp.concatenate(
                [x_ref[par * (lev // 2) + h, 0, :, 0:piece] for h in range(lev // 2)], axis=1
            ).astype(F32)
            code = part_code(pairs_ref, group, wave_count, 0, par, per)
            spread = jnp.concatenate(
                [jnp.where(code == b, value, 0.0) for b in range(2 * GROUP)], axis=0
            ).astype(BF)
            matrix = whole[:, par].reshape(per, half_lat)
            sums.append(jnp.dot(spread, matrix, preferred_element_type=F32))
        tail = x_ref[lev // 2 - 1, 0, :, piece : piece + GROUP].astype(F32)
        lane8 = lax.broadcasted_iota(jnp.int32, (1, GROUP), 1)
        nothing = jnp.zeros((eight, GROUP), F32)
        spread = jnp.concatenate(
            [
                jnp.where(lane8 == b // 2, tail, 0.0) if b % 2 else nothing
                for b in range(2 * GROUP)
            ],
            axis=0,
        ).astype(BF)
        sums[0] = sums[0] + jnp.dot(spread, table_ref[wave_count], preferred_element_type=F32)
        row = lax.broadcasted_iota(jnp.int32, (rows, LANE), 0)
        low = by_slot(row // (2 * eight), pairs_ref, group)
        sign = (1 - 2 * (row // eight % 2 * low % 2)).astype(F32)
        north = sums[0] + sums[1]
        back = LANE - 1 - lax.broadcasted_iota(jnp.int32, (rows, LANE), 1)
        tiles = half_lat // LANE
        for target in range(tiles):
            source = slice((tiles - 1 - target) * LANE, (tiles - target) * LANE)
            south = sign * (sums[0][:, source] - sums[1][:, source])
            south = jnp.take_along_axis(south, back, axis=1)
            upper = north[:, target * LANE : (target + 1) * LANE]
            for b in range(2 * GROUP):
                for f in range(2 * own):
                    at = slice(b * eight + 2 * f, b * eight + 2 * f + 2)
                    place = (f // own, f % own, b // 2, b % 2)
                    out[(*place, slice(None), slice(target * LANE, (target + 1) * LANE))] = upper[at]
                    out[
                        (
                            *place,
                            slice(None),
                            slice(half_lat + target * LANE, half_lat + (target + 1) * LANE),
                        )
                    ] = south[at]

    return pl.pallas_call(
        body,
        name="inverse",
        grid_spec=pltpu.PrefetchScalarGridSpec(
            num_scalar_prefetch=1,
            grid=(groups,),
            in_specs=[
                pl.BlockSpec((lev, 1, eight, lanes), lambda g, *_: (0, g, 0, 0)),
                pl.BlockSpec((row_total, GROUP, half_lat), lambda g, *_: (0, g, 0)),
            ],
            out_specs=pl.BlockSpec(
                (2, own, GROUP, 2, 2, 2 * half_lat), lambda g, *_: (0, 0, g, 0, 0, 0)
            ),
        ),
        out_shape=jax.ShapeDtypeStruct((2, own, slots, 2, 2, 2 * half_lat), F32),
    )(pairs, implicit, table)


def exchange(x, axis):
    return lax.all_to_all(x, axis, 0, 0, tiled=True)


def tiled_local(u, v, t, operator, quadrature, table, couples, project, rebuild, factors):
    lev, lat = lax.axis_size("lev"), lax.axis_size("lat")
    levels, band, lons = u.shape
    own = levels // lev
    slots, row_total, _ = table.shape
    wave_count = row_total - 1
    pairs = lax.dynamic_slice_in_dim(couples, lax.axis_index("lat") * slots, slots)
    flat = jnp.transpose(table, (1, 0, 2))
    waves = wave_rows_call(couples, lons * lev, wave_count)
    received = []
    for lo, hi in CHUNKS:
        products = products_call(u, v, t, operator, lev, lo, hi - lo)
        products = exchange(products, "lev")
        pieces = products.reshape(lev, (hi - lo) * LANE, lons)
        fourier = fourier_call(waves, pieces)
        received.append(exchange(fourier.reshape(lat, slots * 4, -1), "lat"))
    spectral = exchange(forward_call(pairs, received, CHUNKS, flat, quadrature, lev), "lev")
    to_modes, level = mix_matrix(project, own)
    to_levels, _ = mix_matrix(rebuild, own)
    factor_rows = jnp.broadcast_to(factors[level][:, None], (level.shape[0], LANE))
    position = lax.axis_index("lev").astype(jnp.int32)[None]
    implicit = implicit_call(
        pairs, position, spectral, to_modes, to_levels, factor_rows, wave_count
    )
    return inverse_call(pairs, exchange(implicit, "lev"), flat)


def fits(lev, band, lons, levels, slots, row_total, half_lat):
    return (
        lev % 2 == 0
        and levels == 2 * lev
        and band == CHUNKS[-1][1] * SUB
        and lons % LANE == 0
        and slots % GROUP == 0
        and row_total % 2 == 1
        and (row_total - 1) * GROUP % (lev * LANE) == 0
        and half_lat % LANE == 0
    )


def fourier_table(position_wavenumber_couples, lon_count, wave_count):
    repeated = jnp.repeat(position_wavenumber_couples, 4)
    column = jnp.arange(repeated.shape[0], dtype=jnp.int32)
    wavenumber = jnp.where(column // 2 % 2 == 0, repeated, wave_count - 1 - repeated)
    longitude = jnp.arange(lon_count, dtype=jnp.int32)
    phase_index = longitude[:, None] * wavenumber[None, :] % lon_count
    radians = phase_index.astype(jnp.float32) * (2.0 * math.pi / lon_count)
    values = jnp.where(column % 2 == 0, jnp.cos(radians), -jnp.sin(radians)) / math.sqrt(lon_count)
    return values.astype(jnp.bfloat16)


def row_layout(low_waves, wave_count, row_index):
    row_grid = row_index[None, :]
    low_grid = low_waves[:, None]
    boundary = wave_count - low_grid
    second_part = row_grid >= boundary
    parity = jnp.where(second_part, row_grid - boundary, row_grid) % 2
    degree = jnp.where(second_part, row_grid - 1, low_grid + row_grid)
    return (second_part, parity, degree)


def row_selector(second_part, parity):
    choices_two = jnp.arange(2, dtype=jnp.int32)
    parity_hit = parity[..., None] == choices_two
    part_hit = second_part.astype(jnp.int32)[..., None] == choices_two
    return parity_hit[..., :, None] & part_hit[..., None, :]


def damping(degree, eigen_backward_factors, wave_count):
    total = degree.astype(jnp.float32)
    factor = total * (total + 1.0) / float(wave_count * wave_count)
    return 1.0 / (1.0 + factor[:, :, None] * eigen_backward_factors[None, None, :])


def forward_legendre(
    by_wave, associated_polynomial_table, quadrature_factors_north, own_pairs, wave_count
):
    field_count, layer_tally, lat_count, column_count = by_wave.shape
    half_rows = lat_count // 2
    slot_count = column_count // 4
    northern = by_wave[:, :, :half_rows].astype(jnp.float32)
    southern = by_wave[:, :, half_rows:][:, :, ::-1].astype(jnp.float32)
    folded = (
        jnp.stack([northern + southern, northern - southern]) * quadrature_factors_north[:, None]
    )
    folded = folded.astype(jnp.bfloat16).reshape(
        2, field_count, layer_tally, half_rows, slot_count, 2, 2
    )
    folded = jnp.transpose(folded, (4, 3, 0, 5, 6, 1, 2)).reshape(slot_count, half_rows, -1)
    product = jnp.einsum(
        "srl,slc->src", associated_polynomial_table, folded, preferred_element_type=jnp.float32
    )
    product = product.reshape(slot_count, wave_count + 1, 2, 2, 2, field_count, layer_tally)
    layout = row_layout(own_pairs, wave_count, jnp.arange(wave_count + 1, dtype=jnp.int32))
    chosen = row_selector(layout[0], layout[1])
    return jnp.sum(jnp.where(chosen[..., None, None, None], product, 0.0), axis=(2, 3)).astype(
        jnp.bfloat16
    )


def inverse_legendre(implicit, associated_polynomial_table, own_pairs, wave_count):
    slot_count = implicit.shape[0]
    row_total = implicit.shape[1]
    field_count = implicit.shape[3]
    layer_tally = implicit.shape[4]
    layout = row_layout(own_pairs, wave_count, jnp.arange(row_total, dtype=jnp.int32))
    chosen = row_selector(layout[0], layout[1])
    spread = jnp.where(
        chosen[..., None, None, None], implicit[:, :, None, None], jnp.zeros((), implicit.dtype)
    )
    spread = spread.reshape(slot_count, row_total, -1)
    summed = jnp.einsum(
        "srl,src->slc", associated_polynomial_table, spread, preferred_element_type=jnp.float32
    )
    summed = summed.reshape(
        slot_count, associated_polynomial_table.shape[2], 2, 2, 2, field_count, layer_tally
    )
    northern = summed[:, :, 0] + summed[:, :, 1]
    southern = (summed[:, :, 0] - summed[:, :, 1])[:, ::-1]
    latitudes = jnp.concatenate([northern, southern], axis=1)
    return jnp.transpose(latitudes, (4, 5, 0, 2, 3, 1))


def plain_local(
    zonal_velocity,
    meridional_velocity,
    air_warmth,
    pressure_integration_operator,
    quadrature_factors_north,
    associated_polynomial_table,
    position_wavenumber_couples,
    layer_projection_operator,
    eigen_reconstruction_operator,
    eigen_backward_factors,
):
    layer_tally = air_warmth.shape[0]
    gravity_potential_surface = jnp.dot(
        pressure_integration_operator,
        air_warmth.reshape(layer_tally, -1),
        preferred_element_type=jnp.float32,
    )
    gravity_potential_surface = gravity_potential_surface.reshape(air_warmth.shape)
    eastward = zonal_velocity.astype(jnp.float32)
    northward = meridional_velocity.astype(jnp.float32)
    warmth_spectrum_field = air_warmth.astype(jnp.float32)
    products = jnp.stack(
        [
            eastward * northward + gravity_potential_surface,
            (eastward + northward) * warmth_spectrum_field,
        ]
    ).astype(jnp.bfloat16)
    by_level = lax.all_to_all(products, "lev", split_axis=1, concat_axis=3, tiled=True)
    field_count = by_level.shape[0]
    own_levels = by_level.shape[1]
    band_rows = by_level.shape[2]
    lon_count = by_level.shape[3]
    slot_count = associated_polynomial_table.shape[0]
    wave_count = associated_polynomial_table.shape[1] - 1
    row_total = wave_count + 1
    transform = fourier_table(position_wavenumber_couples, lon_count, wave_count)
    harmonic_coefficients_field = jnp.dot(
        by_level.reshape(-1, lon_count), transform, preferred_element_type=jnp.float32
    )
    harmonic_coefficients_field = harmonic_coefficients_field.astype(jnp.bfloat16).reshape(
        field_count, own_levels, band_rows, -1
    )
    by_wave = lax.all_to_all(
        harmonic_coefficients_field, "lat", split_axis=3, concat_axis=2, tiled=True
    )
    own_pairs = lax.dynamic_slice_in_dim(
        position_wavenumber_couples, lax.axis_index("lat") * slot_count, slot_count
    )
    spectral = forward_legendre(
        by_wave, associated_polynomial_table, quadrature_factors_north, own_pairs, wave_count
    )
    group_size = lax.axis_size("lev")
    padded_rows = -(-row_total // group_size) * group_size
    block_rows = padded_rows // group_size
    padded = jnp.pad(spectral, ((0, 0), (0, padded_rows - row_total), (0, 0), (0, 0), (0, 0)))
    received = lax.all_to_all(padded, "lev", split_axis=1, concat_axis=4, tiled=True)
    row_index = lax.axis_index("lev") * block_rows + jnp.arange(block_rows, dtype=jnp.int32)
    degree = row_layout(own_pairs, wave_count, row_index)[2]
    level_total = received.shape[4]
    flat_rows = received.reshape(-1, level_total)
    mode_values = jnp.dot(
        flat_rows, layer_projection_operator.T, preferred_element_type=jnp.float32
    ).reshape(received.shape)
    damped = (
        mode_values * damping(degree, eigen_backward_factors, wave_count)[:, :, None, None, :]
    ).astype(jnp.bfloat16)
    result = jnp.dot(
        damped.reshape(-1, level_total),
        eigen_reconstruction_operator.T,
        preferred_element_type=jnp.float32,
    )
    result = result.reshape(received.shape).astype(jnp.bfloat16)
    implicit = lax.all_to_all(result, "lev", split_axis=4, concat_axis=1, tiled=True)[:, :row_total]
    return inverse_legendre(implicit, associated_polynomial_table, own_pairs, wave_count)


def local(*args):
    table = args[5]
    sizes = args[0].shape
    if fits(
        lax.axis_size("lev"),
        sizes[1],
        sizes[2],
        sizes[0],
        table.shape[0],
        table.shape[1],
        table.shape[2],
    ):
        return tiled_local(*args)
    return plain_local(*args)


def solution(mesh):
    placed = (
        P(None, "lat", "lev"),
        P(None, "lat", "lev"),
        P(None, "lat", "lev"),
        P(),
        P(),
        P("lat", None, None),
        P(),
        P(),
        P(),
        P(),
    )
    return jax.shard_map(
        local,
        mesh=mesh,
        in_specs=placed,
        out_specs=P(None, "lev", "lat", None, None, None),
        check_vma=False,
    )
```

```python
import math

import jax
import jax.numpy as jnp
from jax import lax
from jax.experimental import pallas as pl
from jax.experimental.pallas import tpu as pltpu
from jax.sharding import PartitionSpec as P


BF = jnp.bfloat16
F32 = jnp.float32
LANE = 128
GROUP = 8
SUB = 32
CHUNKS = ((0, 2), (2, 5))
CUT = (1, 2)


def products_call(place, u, v, t, operator, lev, first, count):
    levels, _, lons = u.shape
    own = levels // lev
    split = SUB // 8

    def body(place_ref, op_ref, u_ref, v_ref, t_ref, *rest):
        outs, factors = rest[:lev], rest[lev]

        @pl.when(pl.program_id(0) == 0)
        def _():
            values = op_ref[...].astype(F32)
            for k in range(levels):
                for j in range(levels):
                    factors[k, j] = jnp.broadcast_to(values[k : k + 1, j : j + 1], (8, LANE))

        for tile in range(lons // LANE):
            at = slice(tile * LANE, (tile + 1) * LANE)
            warm = [t_ref[j, :, at].astype(F32).reshape(split, 8, LANE) for j in range(levels)]
            for d in range(lev):
                for own_level in range(own):
                    k = jnp.bitwise_xor(place_ref[0], d) * own + own_level
                    height = factors[k, 0] * warm[0]
                    for j in range(1, levels):
                        height = height + factors[k, j] * warm[j]
                    height = height.reshape(SUB, LANE)
                    east = u_ref[k, :, at].astype(F32)
                    north = v_ref[k, :, at].astype(F32)
                    here = t_ref[k, :, at].astype(F32)
                    outs[d][0, own_level, :, at] = (east * north + height).astype(BF)
                    outs[d][0, own + own_level, :, at] = ((east + north) * here).astype(BF)

    grid_in = pl.BlockSpec((levels, SUB, lons), lambda h, *_: (0, first + h, 0))
    return pl.pallas_call(
        body,
        name="products",
        grid_spec=pltpu.PrefetchScalarGridSpec(
            num_scalar_prefetch=1,
            grid=(count,),
            in_specs=[
                pl.BlockSpec((levels, levels), lambda h, *_: (0, 0)),
                grid_in,
                grid_in,
                grid_in,
            ],
            out_specs=[pl.BlockSpec((1, 2 * own, SUB, lons), lambda h, *_: (h, 0, 0, 0))] * lev,
            scratch_shapes=[pltpu.VMEM((levels, levels, 8, LANE), F32)],
        ),
        out_shape=[jax.ShapeDtypeStruct((count, 2 * own, SUB, lons), BF)] * lev,
    )(place, operator, u, v, t)


def sine_cosine(index, period):
    quarter = period // 4
    turn = (index + period // 8) // quarter
    angle = (index - turn * quarter).astype(F32) * (2.0 * math.pi / period)
    square = angle * angle
    sine = 1.0 / 362880
    for c in (-1.0 / 5040, 1.0 / 120, -1.0 / 6, 1.0):
        sine = sine * square + c
    sine = sine * angle
    cosine = -1.0 / 3628800
    for c in (1.0 / 40320, -1.0 / 720, 1.0 / 24, -0.5, 1.0):
        cosine = cosine * square + c
    odd = turn % 2 == 1
    first = jnp.where(odd, cosine, sine)
    second = jnp.where(odd, sine, cosine)
    turn = turn % 4
    return jnp.where(turn >= 2, -first, first), jnp.where((turn == 1) | (turn == 2), -second, second)


def wave_rows_call(couples, lon_count, wave_count):
    rows = 4 * couples.shape[0]
    block = rows // 4
    chunk = 16
    scale = 1.0 / math.sqrt(lon_count)

    def body(couples_ref, out):
        base = pl.program_id(0) * (block // 4)
        row = lax.broadcasted_iota(jnp.int32, (chunk, LANE), 0)
        lane = lax.broadcasted_iota(jnp.int32, (chunk, LANE), 1)

        def some_rows(index, carry):
            low = jnp.full((chunk, LANE), couples_ref[base + index * (chunk // 4)], jnp.int32)
            for n in range(1, chunk // 4):
                low = jnp.where(row // 4 == n, couples_ref[base + index * (chunk // 4) + n], low)
            wave = jnp.where(row // 2 % 2 == 0, low, wave_count - 1 - low)
            sine, cosine = sine_cosine(wave * lane % lon_count, lon_count)
            s, c = sine_cosine(wave * LANE % lon_count, lon_count)
            is_sine = row % 2 == 1
            a = jnp.where(is_sine, -sine, cosine) * scale
            b = jnp.where(is_sine, cosine, sine) * scale
            at = pl.ds(pl.multiple_of(index * chunk, chunk), chunk)
            for tile in range(lon_count // LANE):
                out[at, tile * LANE : (tile + 1) * LANE] = a.astype(BF)
                a, b = a * c - b * s, b * c + a * s
            return carry

        lax.fori_loop(0, block // chunk, some_rows, 0, unroll=2)

    return pl.pallas_call(
        body,
        name="wave_rows",
        grid_spec=pltpu.PrefetchScalarGridSpec(
            num_scalar_prefetch=1,
            grid=(rows // block,),
            in_specs=[],
            out_specs=pl.BlockSpec((block, lon_count), lambda i, *_: (i, 0)),
        ),
        out_shape=jax.ShapeDtypeStruct((rows, lon_count), BF),
    )(couples)


def fourier_call(place, here, waves, pieces, peers):
    parts = len(pieces)
    rows, lons = pieces[0].shape
    columns = waves.shape[0]
    block = columns // peers

    def body(place_ref, here_ref, w_ref, *refs):
        outs, total = refs[parts : parts + peers], refs[parts + peers]
        for d in range(parts):

            @pl.when(pl.program_id(0) == d)
            def _():
                term = lax.dot_general(
                    w_ref[...], refs[d][...], (((1,), (1,)), ((), ())), preferred_element_type=F32
                )
                if d > 0:
                    term = total[...] + term
                total[...] = term

        @pl.when(pl.program_id(0) == parts - 1)
        def _():
            for e in range(peers):
                start = pl.multiple_of(jnp.bitwise_xor(here_ref[0], e) * block, 16)
                outs[e][...] = total[pl.ds(start, block)].astype(BF)

    return pl.pallas_call(
        body,
        name="fourier",
        grid_spec=pltpu.PrefetchScalarGridSpec(
            num_scalar_prefetch=2,
            grid=(parts,),
            in_specs=[
                pl.BlockSpec((columns, lons), lambda i, p, h: (0, jnp.bitwise_xor(p[0], i)))
            ]
            + [pl.BlockSpec((rows, lons), lambda i, *_: (0, 0))] * parts,
            out_specs=[pl.BlockSpec((block, rows), lambda i, *_: (0, 0))] * peers,
            scratch_shapes=[pltpu.VMEM((columns, rows), F32)],
        ),
        out_shape=[jax.ShapeDtypeStruct((block, rows), BF)] * peers,
    )(place, here, waves, *pieces)


def by_slot(index, pairs, group):
    value = jnp.full(index.shape, pairs[group * GROUP], jnp.int32)
    for s in range(1, GROUP):
        value = jnp.where(index == s, pairs[group * GROUP + s], value)
    return value


def part_code(pairs, group, wave_count, half, par, lanes):
    lane = lax.broadcasted_iota(jnp.int32, (1, lanes), 1)
    slot = lane % GROUP
    r = 2 * (lane // GROUP + half) + par
    low = by_slot(slot, pairs, group)
    return 2 * slot + (r >= wave_count - low).astype(jnp.int32)


def forward_call(pairs, here, received, chunks, table, quadrature, first, groups):
    row_total, _, half_lat = table.shape
    wave_count = row_total - 1
    bands = len(received[0])
    shares = [block for blocks in received for block in blocks]
    units = chunks[-1][1]
    row_block = GROUP * 4
    fields = LANE // SUB
    rows = fields * row_block
    per = wave_count // 2 * GROUP
    where_unit = {}
    for number, (lo, hi) in enumerate(chunks):
        for unit in range(lo, hi):
            where_unit[unit] = (number, unit - lo)

    def body(pairs_ref, here_ref, *refs):
        shared = refs[: len(shares)]
        table_ref, quad_ref, out, spread = refs[len(shares) : len(shares) + 4]
        recv = refs[len(shares) + 4 :]
        group = pl.program_id(0) + first
        mine = pl.ds(pl.multiple_of(group * row_block, row_block), row_block)
        for number in range(len(chunks)):
            for e in range(bands):
                band = jnp.bitwise_xor(here_ref[0], e)
                recv[number][band] = shared[number * bands + e][mine].astype(F32)
        lane = lax.broadcasted_iota(jnp.int32, (row_block, LANE), 1)
        within, place = lane % SUB, lane // SUB
        row = lax.broadcasted_iota(jnp.int32, (row_block, LANE), 0)
        low = by_slot(row // 4, pairs_ref, group)
        second = row // 2 % 2
        signs = [(1 - 2 * ((par + second * low) % 2)).astype(F32) for par in range(2)]

        def tile(band, unit):
            number, local = where_unit[unit]
            return recv[number][band, :, local * LANE : (local + 1) * LANE]

        for target in range(half_lat // LANE):
            at = slice(target * LANE, (target + 1) * LANE)
            north_tiles, south_tiles = [], []
            for d in range(fields):
                beta = fields * target + d
                band, unit = beta // units, beta % units
                north_tiles.append(tile(band, unit))
                south_tiles.append(tile(bands - 1 - band, units - 1 - unit))
            weight = quad_ref[0:1, at]
            for f in range(fields):
                north = jnp.zeros((row_block, LANE), F32)
                south = jnp.zeros((row_block, LANE), F32)
                for d in range(fields):
                    moved = jnp.take_along_axis(north_tiles[d], f * SUB + within, axis=1)
                    north = jnp.where(place == d, moved, north)
                    moved = jnp.take_along_axis(south_tiles[d], f * SUB + SUB - 1 - within, axis=1)
                    south = jnp.where(place == d, moved, south)
                for par in range(2):
                    folded = (north + signs[par] * south) * weight
                    spread[par, f * row_block : (f + 1) * row_block, at] = folded.astype(BF)
        to = lax.broadcasted_iota(jnp.int32, (rows, rows), 0)
        source = lax.broadcasted_iota(jnp.int32, (rows, rows), 1)
        wanted = to // 2 % fields * row_block + to // (2 * fields) * 2 + to % 2
        order = (source == wanted).astype(BF)
        whole = table_ref[0:wave_count].reshape(wave_count // 2, 2, GROUP, half_lat)
        last = table_ref[wave_count]
        out[0, :, 2 * per :] = jnp.zeros((8, LANE), BF)
        for par in range(2):
            field = jnp.dot(order, spread[par], preferred_element_type=F32).astype(BF)
            matrix = whole[:, par].reshape(per, half_lat)
            product = lax.dot_general(
                field, matrix, (((1,), (1,)), ((), ())), preferred_element_type=F32
            )
            code = part_code(pairs_ref, group, wave_count, 0, par, per)
            kept = jnp.zeros((GROUP, per), F32)
            for b in range(2 * GROUP):
                kept = kept + jnp.where(code == b, product[b * 8 : (b + 1) * 8], 0.0)
            out[0, :, par * per : (par + 1) * per] = kept.astype(BF)
            if par == 0:
                ending = lax.dot_general(
                    field, last, (((1,), (1,)), ((), ())), preferred_element_type=F32
                )
                lane8 = lax.broadcasted_iota(jnp.int32, (1, GROUP), 1)
                kept = jnp.zeros((GROUP, GROUP), F32)
                for b in range(GROUP):
                    kept = kept + jnp.where(lane8 == b, ending[b * 16 + 8 : b * 16 + 16], 0.0)
                out[0, :, 2 * per : 2 * per + GROUP] = kept.astype(BF)

    return pl.pallas_call(
        body,
        name="forward",
        grid_spec=pltpu.PrefetchScalarGridSpec(
            num_scalar_prefetch=2,
            grid=(groups,),
            in_specs=[pl.BlockSpec(block.shape, lambda g, *_: (0, 0)) for block in shares]
            + [
                pl.BlockSpec((row_total, GROUP, half_lat), lambda g, *_: (0, first + g, 0)),
                pl.BlockSpec((1, half_lat), lambda g, *_: (0, 0)),
            ],
            out_specs=pl.BlockSpec((1, 8, 2 * per + LANE), lambda g, *_: (g, 0, 0)),
            scratch_shapes=[pltpu.VMEM((2, rows, half_lat), BF)]
            + [pltpu.VMEM((bands, row_block, (hi - lo) * LANE), F32) for lo, hi in chunks],
        ),
        out_shape=jax.ShapeDtypeStruct((groups, 8, 2 * per + LANE), BF),
    )(pairs, here, *shares, table, quadrature[None, :])


def mix_matrix(operator, own):
    levels = operator.shape[0]
    n = levels * 4
    row = jnp.arange(n, dtype=jnp.int32)
    level = row // (4 * own) * own + row // 2 % own
    rest = row // (2 * own) % 2 * 2 + row % 2
    hot = (level[:, None] == jnp.arange(levels)[None, :]).astype(BF)
    spread = jnp.dot(jnp.dot(hot, operator, preferred_element_type=F32).astype(BF), hot.T,
                     preferred_element_type=F32)
    return jnp.where(rest[:, None] == rest[None, :], spread, 0.0).astype(BF), level


def inverse_call(pairs, place, gathered, project, rebuild, factors, table, first, before):
    row_total, slots, half_lat = table.shape
    wave_count = row_total - 1
    lev = len(gathered)
    groups, eight, lanes = gathered[0].shape
    n = lev * eight
    per = wave_count // 2 * GROUP
    rows = 2 * GROUP * eight
    own = eight // 4

    def body(pairs_ref, place_ref, *refs):
        got = refs[:lev]
        p_ref, r_ref, f_ref, table_ref = refs[lev : lev + 4]
        out, stack, x_ref = refs[-3:]
        group = pl.program_id(0) + first
        for d in range(lev):
            stack[jnp.bitwise_xor(place_ref[0], d)] = got[d][0].astype(F32)
        lane = lax.broadcasted_iota(jnp.int32, (1, lanes), 1)
        place = lane // GROUP
        half = wave_count // 2
        r = jnp.where(
            place < half, 2 * place, jnp.where(place < 2 * half, 2 * (place - half) + 1, wave_count)
        )
        low = by_slot(lane % GROUP, pairs_ref, group)
        degree = jnp.where(r >= wave_count - low, r - 1, low + r).astype(F32)
        factor = degree * (degree + 1.0) / float(wave_count * wave_count)
        damping = 1.0 / (1.0 + factor * f_ref[:, 0:1])
        values = stack[...].reshape(n, lanes).astype(BF)
        modes = jnp.dot(p_ref[...], values, preferred_element_type=F32)
        damped = (modes * damping).astype(BF)
        x_ref[...] = jnp.dot(r_ref[...], damped, preferred_element_type=F32).astype(BF)
        whole = table_ref[0:wave_count].reshape(wave_count // 2, 2, GROUP, half_lat)
        sums = []
        for par in range(2):
            value = x_ref[:, par * per : (par + 1) * per].astype(F32)
            code = part_code(pairs_ref, group, wave_count, 0, par, per)
            spread = jnp.concatenate(
                [jnp.where(code == b, value, 0.0) for b in range(2 * GROUP)], axis=0
            ).astype(BF)
            matrix = whole[:, par].reshape(per, half_lat)
            sums.append(jnp.dot(spread, matrix, preferred_element_type=F32))
        tail = x_ref[:, 2 * per : 2 * per + GROUP].astype(F32)
        lane8 = lax.broadcasted_iota(jnp.int32, (1, GROUP), 1)
        nothing = jnp.zeros((eight, GROUP), F32)
        spread = jnp.concatenate(
            [
                jnp.where(lane8 == b // 2, tail, 0.0) if b % 2 else nothing
                for b in range(2 * GROUP)
            ],
            axis=0,
        ).astype(BF)
        sums[0] = sums[0] + jnp.dot(spread, table_ref[wave_count], preferred_element_type=F32)
        row = lax.broadcasted_iota(jnp.int32, (rows, LANE), 0)
        low = by_slot(row // (2 * eight), pairs_ref, group)
        sign = (1 - 2 * (row // eight % 2 * low % 2)).astype(F32)
        north = sums[0] + sums[1]
        back = LANE - 1 - lax.broadcasted_iota(jnp.int32, (rows, LANE), 1)
        tiles = half_lat // LANE
        for target in range(tiles):
            source = slice((tiles - 1 - target) * LANE, (tiles - target) * LANE)
            south = sign * (sums[0][:, source] - sums[1][:, source])
            south = jnp.take_along_axis(south, back, axis=1)
            upper = north[:, target * LANE : (target + 1) * LANE]
            for b in range(2 * GROUP):
                for f in range(2 * own):
                    at = slice(b * eight + 2 * f, b * eight + 2 * f + 2)
                    place = (f // own, f % own, b // 2, b % 2)
                    out[(*place, slice(None), slice(target * LANE, (target + 1) * LANE))] = upper[at]
                    out[
                        (
                            *place,
                            slice(None),
                            slice(half_lat + target * LANE, half_lat + (target + 1) * LANE),
                        )
                    ] = south[at]

    more = () if before is None else (before,)
    return pl.pallas_call(
        body,
        name="inverse",
        grid_spec=pltpu.PrefetchScalarGridSpec(
            num_scalar_prefetch=2,
            grid=(groups,),
            in_specs=[pl.BlockSpec((1, eight, lanes), lambda g, *_: (g, 0, 0))] * lev
            + [
                pl.BlockSpec((n, n), lambda g, *_: (0, 0)),
                pl.BlockSpec((eight, n), lambda g, p, q: (q[0], 0)),
                pl.BlockSpec((n, LANE), lambda g, *_: (0, 0)),
                pl.BlockSpec((row_total, GROUP, half_lat), lambda g, *_: (0, first + g, 0)),
            ]
            + [pl.BlockSpec(memory_space=pl.ANY)] * len(more),
            out_specs=pl.BlockSpec(
                (2, own, GROUP, 2, 2, 2 * half_lat), lambda g, *_: (0, 0, first + g, 0, 0, 0)
            ),
            scratch_shapes=[
                pltpu.VMEM((lev, eight, lanes), F32),
                pltpu.VMEM((eight, lanes), BF),
            ],
        ),
        out_shape=jax.ShapeDtypeStruct((2, own, slots, 2, 2, 2 * half_lat), F32),
        input_output_aliases={lev + 6: 0} if more else {},
    )(pairs, place, *gathered, project, rebuild, factors, table, *more)


def swap(blocks, axis):
    count = len(blocks)
    return [blocks[0]] + [
        lax.ppermute(blocks[d], axis, [(i, i ^ d) for i in range(count)]) for d in range(1, count)
    ]


def tiled_local(u, v, t, operator, quadrature, table, couples, project, rebuild, factors):
    lev, lat = lax.axis_size("lev"), lax.axis_size("lat")
    levels, _, lons = u.shape
    own = levels // lev
    slots, row_total, _ = table.shape
    wave_count = row_total - 1
    place = lax.axis_index("lev").astype(jnp.int32)[None]
    here = lax.axis_index("lat").astype(jnp.int32)[None]
    pairs = lax.dynamic_slice_in_dim(couples, lax.axis_index("lat") * slots, slots)
    flat = jnp.transpose(table, (1, 0, 2))
    received = []
    after = (u, v, t)
    waves = None
    for lo, hi in CHUNKS:
        blocks = products_call(place, *after, operator, lev, lo, hi - lo)
        if waves is None:
            couples, blocks = lax.optimization_barrier((couples, blocks))
            waves = wave_rows_call(couples, lons * lev, wave_count)
            after = lax.optimization_barrier((u, v, t, waves))
            after, waves = after[:3], after[3]
        blocks = swap(blocks, "lev")
        pieces = [x.reshape((hi - lo) * LANE, lons) for x in blocks]
        blocks = fourier_call(place, here, waves, pieces, lat)
        received.append(swap(blocks, "lat"))
    to_modes, level = mix_matrix(project, own)
    to_levels, _ = mix_matrix(rebuild, own)
    factor_rows = jnp.broadcast_to(factors[level][:, None], (level.shape[0], LANE))
    groups = slots // GROUP
    cut = -(-groups * CUT[0] // CUT[1])
    parts = ((0, cut), (cut, groups - cut))
    gathered = []
    for first, count in parts:
        block = forward_call(pairs, here, received, CHUNKS, flat, quadrature, first, count)
        gathered.append(swap([block] * lev, "lev"))
    result = None
    for (first, _), blocks in zip(parts, gathered):
        result = inverse_call(
            pairs, place, blocks, to_modes, to_levels, factor_rows, flat, first, result
        )
    return result


def fits(lev, lat, band, lons, levels, slots, row_total, half_lat):
    return (
        lev % 2 == 0
        and lev & (lev - 1) == 0
        and lat & (lat - 1) == 0
        and lons * lev % 8 == 0
        and levels == 2 * lev
        and band == CHUNKS[-1][1] * SUB
        and lons % LANE == 0
        and slots % GROUP == 0
        and row_total % 2 == 1
        and (row_total - 1) * GROUP % (2 * LANE) == 0
        and half_lat % LANE == 0
    )


def fourier_table(position_wavenumber_couples, lon_count, wave_count):
    repeated = jnp.repeat(position_wavenumber_couples, 4)
    column = jnp.arange(repeated.shape[0], dtype=jnp.int32)
    wavenumber = jnp.where(column // 2 % 2 == 0, repeated, wave_count - 1 - repeated)
    longitude = jnp.arange(lon_count, dtype=jnp.int32)
    phase_index = longitude[:, None] * wavenumber[None, :] % lon_count
    radians = phase_index.astype(jnp.float32) * (2.0 * math.pi / lon_count)
    values = jnp.where(column % 2 == 0, jnp.cos(radians), -jnp.sin(radians)) / math.sqrt(lon_count)
    return values.astype(jnp.bfloat16)


def row_layout(low_waves, wave_count, row_index):
    row_grid = row_index[None, :]
    low_grid = low_waves[:, None]
    boundary = wave_count - low_grid
    second_part = row_grid >= boundary
    parity = jnp.where(second_part, row_grid - boundary, row_grid) % 2
    degree = jnp.where(second_part, row_grid - 1, low_grid + row_grid)
    return (second_part, parity, degree)


def row_selector(second_part, parity):
    choices_two = jnp.arange(2, dtype=jnp.int32)
    parity_hit = parity[..., None] == choices_two
    part_hit = second_part.astype(jnp.int32)[..., None] == choices_two
    return parity_hit[..., :, None] & part_hit[..., None, :]


def damping(degree, eigen_backward_factors, wave_count):
    total = degree.astype(jnp.float32)
    factor = total * (total + 1.0) / float(wave_count * wave_count)
    return 1.0 / (1.0 + factor[:, :, None] * eigen_backward_factors[None, None, :])


def forward_legendre(
    by_wave, associated_polynomial_table, quadrature_factors_north, own_pairs, wave_count
):
    field_count, layer_tally, lat_count, column_count = by_wave.shape
    half_rows = lat_count // 2
    slot_count = column_count // 4
    northern = by_wave[:, :, :half_rows].astype(jnp.float32)
    southern = by_wave[:, :, half_rows:][:, :, ::-1].astype(jnp.float32)
    folded = (
        jnp.stack([northern + southern, northern - southern]) * quadrature_factors_north[:, None]
    )
    folded = folded.astype(jnp.bfloat16).reshape(
        2, field_count, layer_tally, half_rows, slot_count, 2, 2
    )
    folded = jnp.transpose(folded, (4, 3, 0, 5, 6, 1, 2)).reshape(slot_count, half_rows, -1)
    product = jnp.einsum(
        "srl,slc->src", associated_polynomial_table, folded, preferred_element_type=jnp.float32
    )
    product = product.reshape(slot_count, wave_count + 1, 2, 2, 2, field_count, layer_tally)
    layout = row_layout(own_pairs, wave_count, jnp.arange(wave_count + 1, dtype=jnp.int32))
    chosen = row_selector(layout[0], layout[1])
    return jnp.sum(jnp.where(chosen[..., None, None, None], product, 0.0), axis=(2, 3)).astype(
        jnp.bfloat16
    )


def inverse_legendre(implicit, associated_polynomial_table, own_pairs, wave_count):
    slot_count = implicit.shape[0]
    row_total = implicit.shape[1]
    field_count = implicit.shape[3]
    layer_tally = implicit.shape[4]
    layout = row_layout(own_pairs, wave_count, jnp.arange(row_total, dtype=jnp.int32))
    chosen = row_selector(layout[0], layout[1])
    spread = jnp.where(
        chosen[..., None, None, None], implicit[:, :, None, None], jnp.zeros((), implicit.dtype)
    )
    spread = spread.reshape(slot_count, row_total, -1)
    summed = jnp.einsum(
        "srl,src->slc", associated_polynomial_table, spread, preferred_element_type=jnp.float32
    )
    summed = summed.reshape(
        slot_count, associated_polynomial_table.shape[2], 2, 2, 2, field_count, layer_tally
    )
    northern = summed[:, :, 0] + summed[:, :, 1]
    southern = (summed[:, :, 0] - summed[:, :, 1])[:, ::-1]
    latitudes = jnp.concatenate([northern, southern], axis=1)
    return jnp.transpose(latitudes, (4, 5, 0, 2, 3, 1))


def plain_local(
    zonal_velocity,
    meridional_velocity,
    air_warmth,
    pressure_integration_operator,
    quadrature_factors_north,
    associated_polynomial_table,
    position_wavenumber_couples,
    layer_projection_operator,
    eigen_reconstruction_operator,
    eigen_backward_factors,
):
    layer_tally = air_warmth.shape[0]
    gravity_potential_surface = jnp.dot(
        pressure_integration_operator,
        air_warmth.reshape(layer_tally, -1),
        preferred_element_type=jnp.float32,
    )
    gravity_potential_surface = gravity_potential_surface.reshape(air_warmth.shape)
    eastward = zonal_velocity.astype(jnp.float32)
    northward = meridional_velocity.astype(jnp.float32)
    warmth_spectrum_field = air_warmth.astype(jnp.float32)
    products = jnp.stack(
        [
            eastward * northward + gravity_potential_surface,
            (eastward + northward) * warmth_spectrum_field,
        ]
    ).astype(jnp.bfloat16)
    by_level = lax.all_to_all(products, "lev", split_axis=1, concat_axis=3, tiled=True)
    field_count = by_level.shape[0]
    own_levels = by_level.shape[1]
    band_rows = by_level.shape[2]
    lon_count = by_level.shape[3]
    slot_count = associated_polynomial_table.shape[0]
    wave_count = associated_polynomial_table.shape[1] - 1
    row_total = wave_count + 1
    transform = fourier_table(position_wavenumber_couples, lon_count, wave_count)
    harmonic_coefficients_field = jnp.dot(
        by_level.reshape(-1, lon_count), transform, preferred_element_type=jnp.float32
    )
    harmonic_coefficients_field = harmonic_coefficients_field.astype(jnp.bfloat16).reshape(
        field_count, own_levels, band_rows, -1
    )
    by_wave = lax.all_to_all(
        harmonic_coefficients_field, "lat", split_axis=3, concat_axis=2, tiled=True
    )
    own_pairs = lax.dynamic_slice_in_dim(
        position_wavenumber_couples, lax.axis_index("lat") * slot_count, slot_count
    )
    spectral = forward_legendre(
        by_wave, associated_polynomial_table, quadrature_factors_north, own_pairs, wave_count
    )
    group_size = lax.axis_size("lev")
    padded_rows = -(-row_total // group_size) * group_size
    block_rows = padded_rows // group_size
    padded = jnp.pad(spectral, ((0, 0), (0, padded_rows - row_total), (0, 0), (0, 0), (0, 0)))
    received = lax.all_to_all(padded, "lev", split_axis=1, concat_axis=4, tiled=True)
    row_index = lax.axis_index("lev") * block_rows + jnp.arange(block_rows, dtype=jnp.int32)
    degree = row_layout(own_pairs, wave_count, row_index)[2]
    level_total = received.shape[4]
    flat_rows = received.reshape(-1, level_total)
    mode_values = jnp.dot(
        flat_rows, layer_projection_operator.T, preferred_element_type=jnp.float32
    ).reshape(received.shape)
    damped = (
        mode_values * damping(degree, eigen_backward_factors, wave_count)[:, :, None, None, :]
    ).astype(jnp.bfloat16)
    result = jnp.dot(
        damped.reshape(-1, level_total),
        eigen_reconstruction_operator.T,
        preferred_element_type=jnp.float32,
    )
    result = result.reshape(received.shape).astype(jnp.bfloat16)
    implicit = lax.all_to_all(result, "lev", split_axis=4, concat_axis=1, tiled=True)[:, :row_total]
    return inverse_legendre(implicit, associated_polynomial_table, own_pairs, wave_count)


def local(*args):
    table = args[5]
    sizes = args[0].shape
    if fits(
        lax.axis_size("lev"),
        lax.axis_size("lat"),
        sizes[1],
        sizes[2],
        sizes[0],
        table.shape[0],
        table.shape[1],
        table.shape[2],
    ):
        return tiled_local(*args)
    return plain_local(*args)


def solution(mesh):
    placed = (
        P(None, "lat", "lev"),
        P(None, "lat", "lev"),
        P(None, "lat", "lev"),
        P(),
        P(),
        P("lat", None, None),
        P(),
        P(),
        P(),
        P(),
    )
    return jax.shard_map(
        local,
        mesh=mesh,
        in_specs=placed,
        out_specs=P(None, "lev", "lat", None, None, None),
        check_vma=False,
    )
```

```python
import math

import jax
import jax.numpy as jnp
from jax import lax
from jax.experimental import pallas as pl
from jax.experimental.pallas import tpu as pltpu
from jax.sharding import PartitionSpec as P


BF = jnp.bfloat16
F32 = jnp.float32
LANE = 128
GROUP = 8
SUB = 32
CHUNKS = ((0, 2), (2, 5))
CUT = (1, 2)


def products_call(place, u, v, t, operator, lev, first, count):
    levels, _, lons = u.shape
    own = levels // lev
    split = SUB // 8

    def body(place_ref, op_ref, u_ref, v_ref, t_ref, *rest):
        outs, factors = rest[:lev], rest[lev]

        @pl.when(pl.program_id(0) == 0)
        def _():
            values = op_ref[...].astype(F32)
            for k in range(levels):
                for j in range(levels):
                    factors[k, j] = jnp.broadcast_to(values[k : k + 1, j : j + 1], (8, LANE))

        for tile in range(lons // LANE):
            at = slice(tile * LANE, (tile + 1) * LANE)
            warm = [t_ref[j, :, at].astype(F32).reshape(split, 8, LANE) for j in range(levels)]
            for d in range(lev):
                for own_level in range(own):
                    k = jnp.bitwise_xor(place_ref[0], d) * own + own_level
                    height = factors[k, 0] * warm[0]
                    for j in range(1, levels):
                        height = height + factors[k, j] * warm[j]
                    height = height.reshape(SUB, LANE)
                    east = u_ref[k, :, at].astype(F32)
                    north = v_ref[k, :, at].astype(F32)
                    here = t_ref[k, :, at].astype(F32)
                    outs[d][0, own_level, :, at] = (east * north + height).astype(BF)
                    outs[d][0, own + own_level, :, at] = ((east + north) * here).astype(BF)

    grid_in = pl.BlockSpec((levels, SUB, lons), lambda h, *_: (0, first + h, 0))
    return pl.pallas_call(
        body,
        name="products",
        grid_spec=pltpu.PrefetchScalarGridSpec(
            num_scalar_prefetch=1,
            grid=(count,),
            in_specs=[
                pl.BlockSpec((levels, levels), lambda h, *_: (0, 0)),
                grid_in,
                grid_in,
                grid_in,
            ],
            out_specs=[pl.BlockSpec((1, 2 * own, SUB, lons), lambda h, *_: (h, 0, 0, 0))] * lev,
            scratch_shapes=[pltpu.VMEM((levels, levels, 8, LANE), F32)],
        ),
        out_shape=[jax.ShapeDtypeStruct((count, 2 * own, SUB, lons), BF)] * lev,
    )(place, operator, u, v, t)


def whole_part(index, period):
    return ((index.astype(F32) + 0.5) * (1.0 / period)).astype(jnp.int32)


def sine_cosine(index, period):
    quarter = period // 4
    index = index - whole_part(index, period) * period
    turn = whole_part(index + period // 8, quarter)
    angle = (index - turn * quarter).astype(F32) * (2.0 * math.pi / period)
    square = angle * angle
    sine = 1.0 / 362880
    for c in (-1.0 / 5040, 1.0 / 120, -1.0 / 6, 1.0):
        sine = sine * square + c
    sine = sine * angle
    cosine = -1.0 / 3628800
    for c in (1.0 / 40320, -1.0 / 720, 1.0 / 24, -0.5, 1.0):
        cosine = cosine * square + c
    odd = (turn == 1) | (turn == 3)
    first = jnp.where(odd, cosine, sine)
    second = jnp.where(odd, sine, cosine)
    minus = (turn == 2) | (turn == 3)
    return jnp.where(minus, -first, first), jnp.where((turn == 1) | (turn == 2), -second, second)


def wave_rows_call(couples, lon_count, wave_count):
    rows = 4 * couples.shape[0]
    block = rows // 4
    chunk = 32
    scale = 1.0 / math.sqrt(lon_count)

    def body(couples_ref, out):
        base = pl.program_id(0) * (block // 4)
        row = lax.broadcasted_iota(jnp.int32, (chunk, LANE), 0)
        lane = lax.broadcasted_iota(jnp.int32, (chunk, LANE), 1)

        def some_rows(index, carry):
            low = jnp.full((chunk, LANE), couples_ref[base + index * (chunk // 4)], jnp.int32)
            for n in range(1, chunk // 4):
                low = jnp.where(row // 4 == n, couples_ref[base + index * (chunk // 4) + n], low)
            wave = jnp.where(row // 2 % 2 == 0, low, wave_count - 1 - low)
            sine, cosine = sine_cosine(wave * lane, lon_count)
            s, c = sine_cosine(wave * LANE, lon_count)
            is_sine = row % 2 == 1
            a = jnp.where(is_sine, -sine, cosine) * scale
            b = jnp.where(is_sine, cosine, sine) * scale
            at = pl.ds(pl.multiple_of(index * chunk, chunk), chunk)
            for tile in range(lon_count // LANE):
                out[at, tile * LANE : (tile + 1) * LANE] = a.astype(BF)
                a, b = a * c - b * s, b * c + a * s
            return carry

        lax.fori_loop(0, block // chunk, some_rows, 0, unroll=2)

    return pl.pallas_call(
        body,
        name="wave_rows",
        grid_spec=pltpu.PrefetchScalarGridSpec(
            num_scalar_prefetch=1,
            grid=(rows // block,),
            in_specs=[],
            out_specs=pl.BlockSpec((block, lon_count), lambda i, *_: (i, 0)),
        ),
        out_shape=jax.ShapeDtypeStruct((rows, lon_count), BF),
    )(couples)


def fourier_call(place, here, waves, pieces, peers):
    parts = len(pieces)
    rows, lons = pieces[0].shape
    columns = waves.shape[0]
    block = columns // peers

    def body(place_ref, here_ref, w_ref, *refs):
        outs, total = refs[parts : parts + peers], refs[parts + peers]
        for d in range(parts):

            @pl.when(pl.program_id(0) == d)
            def _():
                term = lax.dot_general(
                    w_ref[...], refs[d][...], (((1,), (1,)), ((), ())), preferred_element_type=F32
                )
                if d > 0:
                    term = total[...] + term
                total[...] = term

        @pl.when(pl.program_id(0) == parts - 1)
        def _():
            for e in range(peers):
                start = pl.multiple_of(jnp.bitwise_xor(here_ref[0], e) * block, 16)
                outs[e][...] = total[pl.ds(start, block)].astype(BF)

    return pl.pallas_call(
        body,
        name="fourier",
        grid_spec=pltpu.PrefetchScalarGridSpec(
            num_scalar_prefetch=2,
            grid=(parts,),
            in_specs=[
                pl.BlockSpec((columns, lons), lambda i, p, h: (0, jnp.bitwise_xor(p[0], i)))
            ]
            + [pl.BlockSpec((rows, lons), lambda i, *_: (0, 0))] * parts,
            out_specs=[pl.BlockSpec((block, rows), lambda i, *_: (0, 0))] * peers,
            scratch_shapes=[pltpu.VMEM((columns, rows), F32)],
        ),
        out_shape=[jax.ShapeDtypeStruct((block, rows), BF)] * peers,
    )(place, here, waves, *pieces)


def by_slot(index, pairs, group):
    value = jnp.full(index.shape, pairs[group * GROUP], jnp.int32)
    for s in range(1, GROUP):
        value = jnp.where(index == s, pairs[group * GROUP + s], value)
    return value


def across(tiles, place):
    tiles = list(tiles)
    count = len(tiles)
    step = count // 2
    while step:
        shift = step * (LANE // count)
        upper = place // step % 2 == 1
        for d in range(count):
            if d // step % 2 == 0:
                low, high = tiles[d], tiles[d + step]
                tiles[d] = jnp.where(upper, pltpu.roll(high, shift, 1), low)
                tiles[d + step] = jnp.where(upper, high, pltpu.roll(low, LANE - shift, 1))
        step //= 2
    return tiles


def part_code(pairs, group, wave_count, half, par, lanes):
    lane = lax.broadcasted_iota(jnp.int32, (1, lanes), 1)
    slot = lane % GROUP
    r = 2 * (lane // GROUP + half) + par
    low = by_slot(slot, pairs, group)
    return 2 * slot + (r >= wave_count - low).astype(jnp.int32)


def forward_call(pairs, here, received, chunks, table, quadrature, first, groups):
    row_total, _, half_lat = table.shape
    wave_count = row_total - 1
    bands = len(received[0])
    shares = [block for blocks in received for block in blocks]
    units = chunks[-1][1]
    row_block = GROUP * 4
    fields = LANE // SUB
    rows = fields * row_block
    per = wave_count // 2 * GROUP
    where_unit = {}
    for number, (lo, hi) in enumerate(chunks):
        for unit in range(lo, hi):
            where_unit[unit] = (number, unit - lo)

    def body(pairs_ref, here_ref, *refs):
        shared = refs[: len(shares)]
        table_ref, quad_ref, out, spread = refs[len(shares) : len(shares) + 4]
        recv = refs[len(shares) + 4 :]
        group = pl.program_id(0) + first
        mine = pl.ds(pl.multiple_of(group * row_block, row_block), row_block)
        for number in range(len(chunks)):
            for e in range(bands):
                band = jnp.bitwise_xor(here_ref[0], e)
                recv[number][band] = shared[number * bands + e][mine]
        lane = lax.broadcasted_iota(jnp.int32, (row_block, LANE), 1)
        place = lane // SUB
        turned = place * SUB + SUB - 1 - lane % SUB
        row = lax.broadcasted_iota(jnp.int32, (row_block, LANE), 0)
        low = by_slot(row // 4, pairs_ref, group)
        second = row // 2 % 2
        signs = [(1 - 2 * ((par + second * low) % 2)).astype(F32) for par in range(2)]

        def tile(band, unit):
            number, local = where_unit[unit]
            return recv[number][band, :, local * LANE : (local + 1) * LANE]

        for target in range(half_lat // LANE):
            at = slice(target * LANE, (target + 1) * LANE)
            north_tiles, south_tiles = [], []
            for d in range(fields):
                beta = fields * target + d
                band, unit = beta // units, beta % units
                north_tiles.append(tile(band, unit))
                south_tiles.append(tile(bands - 1 - band, units - 1 - unit))
            north_tiles, south_tiles = across(north_tiles, place), across(south_tiles, place)
            weight = quad_ref[0:1, at]
            for f in range(fields):
                north = north_tiles[f].astype(F32)
                south = jnp.take_along_axis(south_tiles[f].astype(F32), turned, axis=1)
                for par in range(2):
                    folded = (north + signs[par] * south) * weight
                    spread[par, f * row_block : (f + 1) * row_block, at] = folded.astype(BF)
        to = lax.broadcasted_iota(jnp.int32, (rows, rows), 0)
        source = lax.broadcasted_iota(jnp.int32, (rows, rows), 1)
        wanted = to // 2 % fields * row_block + to // (2 * fields) * 2 + to % 2
        order = (source == wanted).astype(BF)
        whole = table_ref[0:wave_count].reshape(wave_count // 2, 2, GROUP, half_lat)
        last = table_ref[wave_count]
        out[0, :, 2 * per :] = jnp.zeros((8, LANE), BF)
        for par in range(2):
            field = jnp.dot(order, spread[par], preferred_element_type=F32).astype(BF)
            matrix = whole[:, par].reshape(per, half_lat)
            product = lax.dot_general(
                field, matrix, (((1,), (1,)), ((), ())), preferred_element_type=F32
            )
            code = part_code(pairs_ref, group, wave_count, 0, par, per)
            kept = jnp.zeros((GROUP, per), F32)
            for b in range(2 * GROUP):
                kept = kept + jnp.where(code == b, product[b * 8 : (b + 1) * 8], 0.0)
            out[0, :, par * per : (par + 1) * per] = kept.astype(BF)
            if par == 0:
                ending = lax.dot_general(
                    field, last, (((1,), (1,)), ((), ())), preferred_element_type=F32
                )
                lane8 = lax.broadcasted_iota(jnp.int32, (1, GROUP), 1)
                kept = jnp.zeros((GROUP, GROUP), F32)
                for b in range(GROUP):
                    kept = kept + jnp.where(lane8 == b, ending[b * 16 + 8 : b * 16 + 16], 0.0)
                out[0, :, 2 * per : 2 * per + GROUP] = kept.astype(BF)

    return pl.pallas_call(
        body,
        name="forward",
        grid_spec=pltpu.PrefetchScalarGridSpec(
            num_scalar_prefetch=2,
            grid=(groups,),
            in_specs=[pl.BlockSpec(block.shape, lambda g, *_: (0, 0)) for block in shares]
            + [
                pl.BlockSpec((row_total, GROUP, half_lat), lambda g, *_: (0, first + g, 0)),
                pl.BlockSpec((1, half_lat), lambda g, *_: (0, 0)),
            ],
            out_specs=pl.BlockSpec((1, 8, 2 * per + LANE), lambda g, *_: (g, 0, 0)),
            scratch_shapes=[pltpu.VMEM((2, rows, half_lat), BF)]
            + [pltpu.VMEM((bands, row_block, (hi - lo) * LANE), BF) for lo, hi in chunks],
        ),
        out_shape=jax.ShapeDtypeStruct((groups, 8, 2 * per + LANE), BF),
    )(pairs, here, *shares, table, quadrature[None, :])


def mix_matrix(operator, own):
    levels = operator.shape[0]
    n = levels * 4
    row = jnp.arange(n, dtype=jnp.int32)
    level = row // (4 * own) * own + row // 2 % own
    rest = row // (2 * own) % 2 * 2 + row % 2
    hot = (level[:, None] == jnp.arange(levels)[None, :]).astype(BF)
    spread = jnp.dot(jnp.dot(hot, operator, preferred_element_type=F32).astype(BF), hot.T,
                     preferred_element_type=F32)
    return jnp.where(rest[:, None] == rest[None, :], spread, 0.0).astype(BF), level


def inverse_call(pairs, place, gathered, project, rebuild, factors, table, first, before):
    row_total, slots, half_lat = table.shape
    wave_count = row_total - 1
    lev = len(gathered)
    groups, eight, lanes = gathered[0].shape
    n = lev * eight
    per = wave_count // 2 * GROUP
    rows = 2 * GROUP * eight
    own = eight // 4

    def body(pairs_ref, place_ref, *refs):
        got = refs[:lev]
        p_ref, r_ref, f_ref, table_ref = refs[lev : lev + 4]
        out, stack, x_ref = refs[-3:]
        group = pl.program_id(0) + first
        for d in range(lev):
            stack[jnp.bitwise_xor(place_ref[0], d)] = got[d][0].astype(F32)
        lane = lax.broadcasted_iota(jnp.int32, (1, lanes), 1)
        place = lane // GROUP
        half = wave_count // 2
        r = jnp.where(
            place < half, 2 * place, jnp.where(place < 2 * half, 2 * (place - half) + 1, wave_count)
        )
        low = by_slot(lane % GROUP, pairs_ref, group)
        degree = jnp.where(r >= wave_count - low, r - 1, low + r).astype(F32)
        factor = degree * (degree + 1.0) / float(wave_count * wave_count)
        damping = 1.0 / (1.0 + factor * f_ref[:, 0:1])
        values = stack[...].reshape(n, lanes).astype(BF)
        modes = jnp.dot(p_ref[...], values, preferred_element_type=F32)
        damped = (modes * damping).astype(BF)
        x_ref[...] = jnp.dot(r_ref[...], damped, preferred_element_type=F32).astype(BF)
        whole = table_ref[0:wave_count].reshape(wave_count // 2, 2, GROUP, half_lat)
        sums = []
        for par in range(2):
            value = x_ref[:, par * per : (par + 1) * per].astype(F32)
            code = part_code(pairs_ref, group, wave_count, 0, par, per)
            spread = jnp.concatenate(
                [jnp.where(code == b, value, 0.0) for b in range(2 * GROUP)], axis=0
            ).astype(BF)
            matrix = whole[:, par].reshape(per, half_lat)
            sums.append(jnp.dot(spread, matrix, preferred_element_type=F32))
        tail = x_ref[:, 2 * per : 2 * per + GROUP].astype(F32)
        lane8 = lax.broadcasted_iota(jnp.int32, (1, GROUP), 1)
        nothing = jnp.zeros((eight, GROUP), F32)
        spread = jnp.concatenate(
            [
                jnp.where(lane8 == b // 2, tail, 0.0) if b % 2 else nothing
                for b in range(2 * GROUP)
            ],
            axis=0,
        ).astype(BF)
        sums[0] = sums[0] + jnp.dot(spread, table_ref[wave_count], preferred_element_type=F32)
        row = lax.broadcasted_iota(jnp.int32, (rows, LANE), 0)
        low = by_slot(row // (2 * eight), pairs_ref, group)
        sign = (1 - 2 * (row // eight % 2 * low % 2)).astype(F32)
        north = sums[0] + sums[1]
        back = LANE - 1 - lax.broadcasted_iota(jnp.int32, (rows, LANE), 1)
        tiles = half_lat // LANE
        for target in range(tiles):
            source = slice((tiles - 1 - target) * LANE, (tiles - target) * LANE)
            south = sign * (sums[0][:, source] - sums[1][:, source])
            south = jnp.take_along_axis(south, back, axis=1)
            upper = north[:, target * LANE : (target + 1) * LANE]
            for b in range(2 * GROUP):
                for f in range(2 * own):
                    at = slice(b * eight + 2 * f, b * eight + 2 * f + 2)
                    place = (f // own, f % own, b // 2, b % 2)
                    out[(*place, slice(None), slice(target * LANE, (target + 1) * LANE))] = upper[at]
                    out[
                        (
                            *place,
                            slice(None),
                            slice(half_lat + target * LANE, half_lat + (target + 1) * LANE),
                        )
                    ] = south[at]

    more = () if before is None else (before,)
    return pl.pallas_call(
        body,
        name="inverse",
        grid_spec=pltpu.PrefetchScalarGridSpec(
            num_scalar_prefetch=2,
            grid=(groups,),
            in_specs=[pl.BlockSpec((1, eight, lanes), lambda g, *_: (g, 0, 0))] * lev
            + [
                pl.BlockSpec((n, n), lambda g, *_: (0, 0)),
                pl.BlockSpec((eight, n), lambda g, p, q: (q[0], 0)),
                pl.BlockSpec((n, LANE), lambda g, *_: (0, 0)),
                pl.BlockSpec((row_total, GROUP, half_lat), lambda g, *_: (0, first + g, 0)),
            ]
            + [pl.BlockSpec(memory_space=pl.ANY)] * len(more),
            out_specs=pl.BlockSpec(
                (2, own, GROUP, 2, 2, 2 * half_lat), lambda g, *_: (0, 0, first + g, 0, 0, 0)
            ),
            scratch_shapes=[
                pltpu.VMEM((lev, eight, lanes), F32),
                pltpu.VMEM((eight, lanes), BF),
            ],
        ),
        out_shape=jax.ShapeDtypeStruct((2, own, slots, 2, 2, 2 * half_lat), F32),
        input_output_aliases={lev + 6: 0} if more else {},
    )(pairs, place, *gathered, project, rebuild, factors, table, *more)


def swap(blocks, axis):
    count = len(blocks)
    return [blocks[0]] + [
        lax.ppermute(blocks[d], axis, [(i, i ^ d) for i in range(count)]) for d in range(1, count)
    ]


def tiled_local(u, v, t, operator, quadrature, table, couples, project, rebuild, factors):
    lev, lat = lax.axis_size("lev"), lax.axis_size("lat")
    levels, _, lons = u.shape
    own = levels // lev
    slots, row_total, _ = table.shape
    wave_count = row_total - 1
    place = lax.axis_index("lev").astype(jnp.int32)[None]
    here = lax.axis_index("lat").astype(jnp.int32)[None]
    flat = jnp.transpose(table, (1, 0, 2))
    received = []
    products = []
    for lo, hi in CHUNKS:
        products.append(products_call(place, u, v, t, operator, lev, lo, hi - lo))
    couples, products[-1] = lax.optimization_barrier((couples, products[-1]))
    waves = wave_rows_call(couples, lons * lev, wave_count)
    for (lo, hi), blocks in zip(CHUNKS, products):
        blocks = swap(blocks, "lev")
        pieces = [x.reshape((hi - lo) * LANE, lons) for x in blocks]
        blocks = fourier_call(place, here, waves, pieces, lat)
        if hi == CHUNKS[-1][1]:
            blocks, late = lax.optimization_barrier(
                (blocks, (couples, quadrature, project, rebuild, factors))
            )
        received.append(swap(blocks, "lat"))
    couples, quadrature, project, rebuild, factors = late
    pairs = lax.dynamic_slice_in_dim(couples, lax.axis_index("lat") * slots, slots)
    to_modes, level = mix_matrix(project, own)
    to_levels, _ = mix_matrix(rebuild, own)
    factor_rows = jnp.broadcast_to(factors[level][:, None], (level.shape[0], LANE))
    received, to_modes, to_levels, factor_rows = lax.optimization_barrier(
        (received, to_modes, to_levels, factor_rows)
    )
    groups = slots // GROUP
    cut = -(-groups * CUT[0] // CUT[1])
    parts = ((0, cut), (cut, groups - cut))
    gathered = []
    for first, count in parts:
        block = forward_call(pairs, here, received, CHUNKS, flat, quadrature, first, count)
        gathered.append(swap([block] * lev, "lev"))
    result = None
    for (first, _), blocks in zip(parts, gathered):
        result = inverse_call(
            pairs, place, blocks, to_modes, to_levels, factor_rows, flat, first, result
        )
    return result


def fits(lev, lat, band, lons, levels, slots, row_total, half_lat):
    return (
        lev % 2 == 0
        and lev & (lev - 1) == 0
        and lat & (lat - 1) == 0
        and lons * lev % 8 == 0
        and 2 * (row_total - 1) * LANE < 2**8 * lons * lev
        and levels == 2 * lev
        and band == CHUNKS[-1][1] * SUB
        and lons % LANE == 0
        and slots % GROUP == 0
        and row_total % 2 == 1
        and (row_total - 1) * GROUP % (2 * LANE) == 0
        and half_lat % LANE == 0
    )


def fourier_table(position_wavenumber_couples, lon_count, wave_count):
    repeated = jnp.repeat(position_wavenumber_couples, 4)
    column = jnp.arange(repeated.shape[0], dtype=jnp.int32)
    wavenumber = jnp.where(column // 2 % 2 == 0, repeated, wave_count - 1 - repeated)
    longitude = jnp.arange(lon_count, dtype=jnp.int32)
    phase_index = longitude[:, None] * wavenumber[None, :] % lon_count
    radians = phase_index.astype(jnp.float32) * (2.0 * math.pi / lon_count)
    values = jnp.where(column % 2 == 0, jnp.cos(radians), -jnp.sin(radians)) / math.sqrt(lon_count)
    return values.astype(jnp.bfloat16)


def row_layout(low_waves, wave_count, row_index):
    row_grid = row_index[None, :]
    low_grid = low_waves[:, None]
    boundary = wave_count - low_grid
    second_part = row_grid >= boundary
    parity = jnp.where(second_part, row_grid - boundary, row_grid) % 2
    degree = jnp.where(second_part, row_grid - 1, low_grid + row_grid)
    return (second_part, parity, degree)


def row_selector(second_part, parity):
    choices_two = jnp.arange(2, dtype=jnp.int32)
    parity_hit = parity[..., None] == choices_two
    part_hit = second_part.astype(jnp.int32)[..., None] == choices_two
    return parity_hit[..., :, None] & part_hit[..., None, :]


def damping(degree, eigen_backward_factors, wave_count):
    total = degree.astype(jnp.float32)
    factor = total * (total + 1.0) / float(wave_count * wave_count)
    return 1.0 / (1.0 + factor[:, :, None] * eigen_backward_factors[None, None, :])


def forward_legendre(
    by_wave, associated_polynomial_table, quadrature_factors_north, own_pairs, wave_count
):
    field_count, layer_tally, lat_count, column_count = by_wave.shape
    half_rows = lat_count // 2
    slot_count = column_count // 4
    northern = by_wave[:, :, :half_rows].astype(jnp.float32)
    southern = by_wave[:, :, half_rows:][:, :, ::-1].astype(jnp.float32)
    folded = (
        jnp.stack([northern + southern, northern - southern]) * quadrature_factors_north[:, None]
    )
    folded = folded.astype(jnp.bfloat16).reshape(
        2, field_count, layer_tally, half_rows, slot_count, 2, 2
    )
    folded = jnp.transpose(folded, (4, 3, 0, 5, 6, 1, 2)).reshape(slot_count, half_rows, -1)
    product = jnp.einsum(
        "srl,slc->src", associated_polynomial_table, folded, preferred_element_type=jnp.float32
    )
    product = product.reshape(slot_count, wave_count + 1, 2, 2, 2, field_count, layer_tally)
    layout = row_layout(own_pairs, wave_count, jnp.arange(wave_count + 1, dtype=jnp.int32))
    chosen = row_selector(layout[0], layout[1])
    return jnp.sum(jnp.where(chosen[..., None, None, None], product, 0.0), axis=(2, 3)).astype(
        jnp.bfloat16
    )


def inverse_legendre(implicit, associated_polynomial_table, own_pairs, wave_count):
    slot_count = implicit.shape[0]
    row_total = implicit.shape[1]
    field_count = implicit.shape[3]
    layer_tally = implicit.shape[4]
    layout = row_layout(own_pairs, wave_count, jnp.arange(row_total, dtype=jnp.int32))
    chosen = row_selector(layout[0], layout[1])
    spread = jnp.where(
        chosen[..., None, None, None], implicit[:, :, None, None], jnp.zeros((), implicit.dtype)
    )
    spread = spread.reshape(slot_count, row_total, -1)
    summed = jnp.einsum(
        "srl,src->slc", associated_polynomial_table, spread, preferred_element_type=jnp.float32
    )
    summed = summed.reshape(
        slot_count, associated_polynomial_table.shape[2], 2, 2, 2, field_count, layer_tally
    )
    northern = summed[:, :, 0] + summed[:, :, 1]
    southern = (summed[:, :, 0] - summed[:, :, 1])[:, ::-1]
    latitudes = jnp.concatenate([northern, southern], axis=1)
    return jnp.transpose(latitudes, (4, 5, 0, 2, 3, 1))


def plain_local(
    zonal_velocity,
    meridional_velocity,
    air_warmth,
    pressure_integration_operator,
    quadrature_factors_north,
    associated_polynomial_table,
    position_wavenumber_couples,
    layer_projection_operator,
    eigen_reconstruction_operator,
    eigen_backward_factors,
):
    layer_tally = air_warmth.shape[0]
    gravity_potential_surface = jnp.dot(
        pressure_integration_operator,
        air_warmth.reshape(layer_tally, -1),
        preferred_element_type=jnp.float32,
    )
    gravity_potential_surface = gravity_potential_surface.reshape(air_warmth.shape)
    eastward = zonal_velocity.astype(jnp.float32)
    northward = meridional_velocity.astype(jnp.float32)
    warmth_spectrum_field = air_warmth.astype(jnp.float32)
    products = jnp.stack(
        [
            eastward * northward + gravity_potential_surface,
            (eastward + northward) * warmth_spectrum_field,
        ]
    ).astype(jnp.bfloat16)
    by_level = lax.all_to_all(products, "lev", split_axis=1, concat_axis=3, tiled=True)
    field_count = by_level.shape[0]
    own_levels = by_level.shape[1]
    band_rows = by_level.shape[2]
    lon_count = by_level.shape[3]
    slot_count = associated_polynomial_table.shape[0]
    wave_count = associated_polynomial_table.shape[1] - 1
    row_total = wave_count + 1
    transform = fourier_table(position_wavenumber_couples, lon_count, wave_count)
    harmonic_coefficients_field = jnp.dot(
        by_level.reshape(-1, lon_count), transform, preferred_element_type=jnp.float32
    )
    harmonic_coefficients_field = harmonic_coefficients_field.astype(jnp.bfloat16).reshape(
        field_count, own_levels, band_rows, -1
    )
    by_wave = lax.all_to_all(
        harmonic_coefficients_field, "lat", split_axis=3, concat_axis=2, tiled=True
    )
    own_pairs = lax.dynamic_slice_in_dim(
        position_wavenumber_couples, lax.axis_index("lat") * slot_count, slot_count
    )
    spectral = forward_legendre(
        by_wave, associated_polynomial_table, quadrature_factors_north, own_pairs, wave_count
    )
    group_size = lax.axis_size("lev")
    padded_rows = -(-row_total // group_size) * group_size
    block_rows = padded_rows // group_size
    padded = jnp.pad(spectral, ((0, 0), (0, padded_rows - row_total), (0, 0), (0, 0), (0, 0)))
    received = lax.all_to_all(padded, "lev", split_axis=1, concat_axis=4, tiled=True)
    row_index = lax.axis_index("lev") * block_rows + jnp.arange(block_rows, dtype=jnp.int32)
    degree = row_layout(own_pairs, wave_count, row_index)[2]
    level_total = received.shape[4]
    flat_rows = received.reshape(-1, level_total)
    mode_values = jnp.dot(
        flat_rows, layer_projection_operator.T, preferred_element_type=jnp.float32
    ).reshape(received.shape)
    damped = (
        mode_values * damping(degree, eigen_backward_factors, wave_count)[:, :, None, None, :]
    ).astype(jnp.bfloat16)
    result = jnp.dot(
        damped.reshape(-1, level_total),
        eigen_reconstruction_operator.T,
        preferred_element_type=jnp.float32,
    )
    result = result.reshape(received.shape).astype(jnp.bfloat16)
    implicit = lax.all_to_all(result, "lev", split_axis=4, concat_axis=1, tiled=True)[:, :row_total]
    return inverse_legendre(implicit, associated_polynomial_table, own_pairs, wave_count)


def local(*args):
    table = args[5]
    sizes = args[0].shape
    if fits(
        lax.axis_size("lev"),
        lax.axis_size("lat"),
        sizes[1],
        sizes[2],
        sizes[0],
        table.shape[0],
        table.shape[1],
        table.shape[2],
    ):
        return tiled_local(*args)
    return plain_local(*args)


def solution(mesh):
    placed = (
        P(None, "lat", "lev"),
        P(None, "lat", "lev"),
        P(None, "lat", "lev"),
        P(),
        P(),
        P("lat", None, None),
        P(),
        P(),
        P(),
        P(),
    )
    return jax.shard_map(
        local,
        mesh=mesh,
        in_specs=placed,
        out_specs=P(None, "lev", "lat", None, None, None),
        check_vma=False,
    )
```

```python
import math

import jax
import jax.numpy as jnp
from jax import lax
from jax.experimental import pallas as pl
from jax.experimental.pallas import tpu as pltpu
from jax.sharding import PartitionSpec as P


BF = jnp.bfloat16
F32 = jnp.float32
LANE = 128
GROUP = 8
SUB = 32
CHUNKS = ((0, 2), (2, 5))
CUT = (1, 2)


def products_call(place, u, v, t, operator, lev, first, count):
    levels, _, lons = u.shape
    own = levels // lev
    split = SUB // 8

    def body(place_ref, op_ref, u_ref, v_ref, t_ref, *rest):
        outs, factors = rest[:lev], rest[lev]

        @pl.when(pl.program_id(0) == 0)
        def _():
            values = op_ref[...].astype(F32)
            for k in range(levels):
                for j in range(levels):
                    factors[k, j] = jnp.broadcast_to(values[k : k + 1, j : j + 1], (8, LANE))

        for tile in range(lons // LANE):
            at = slice(tile * LANE, (tile + 1) * LANE)
            warm = [t_ref[j, :, at].astype(F32).reshape(split, 8, LANE) for j in range(levels)]
            for d in range(lev):
                for own_level in range(own):
                    k = jnp.bitwise_xor(place_ref[0], d) * own + own_level
                    height = factors[k, 0] * warm[0]
                    for j in range(1, levels):
                        height = height + factors[k, j] * warm[j]
                    height = height.reshape(SUB, LANE)
                    east = u_ref[k, :, at].astype(F32)
                    north = v_ref[k, :, at].astype(F32)
                    here = t_ref[k, :, at].astype(F32)
                    outs[d][0, own_level, :, at] = (east * north + height).astype(BF)
                    outs[d][0, own + own_level, :, at] = ((east + north) * here).astype(BF)

    grid_in = pl.BlockSpec((levels, SUB, lons), lambda h, *_: (0, first + h, 0))
    return pl.pallas_call(
        body,
        name="products",
        grid_spec=pltpu.PrefetchScalarGridSpec(
            num_scalar_prefetch=1,
            grid=(count,),
            in_specs=[
                pl.BlockSpec((levels, levels), lambda h, *_: (0, 0)),
                grid_in,
                grid_in,
                grid_in,
            ],
            out_specs=[pl.BlockSpec((1, 2 * own, SUB, lons), lambda h, *_: (h, 0, 0, 0))] * lev,
            scratch_shapes=[pltpu.VMEM((levels, levels, 8, LANE), F32)],
        ),
        out_shape=[jax.ShapeDtypeStruct((count, 2 * own, SUB, lons), BF)] * lev,
    )(place, operator, u, v, t)


def whole_part(index, period):
    return ((index.astype(F32) + 0.5) * (1.0 / period)).astype(jnp.int32)


def sine_cosine(index, period):
    quarter = period // 4
    index = index - whole_part(index, period) * period
    turn = whole_part(index + period // 8, quarter)
    angle = (index - turn * quarter).astype(F32) * (2.0 * math.pi / period)
    square = angle * angle
    sine = 1.0 / 362880
    for c in (-1.0 / 5040, 1.0 / 120, -1.0 / 6, 1.0):
        sine = sine * square + c
    sine = sine * angle
    cosine = -1.0 / 3628800
    for c in (1.0 / 40320, -1.0 / 720, 1.0 / 24, -0.5, 1.0):
        cosine = cosine * square + c
    odd = (turn == 1) | (turn == 3)
    first = jnp.where(odd, cosine, sine)
    second = jnp.where(odd, sine, cosine)
    minus = (turn == 2) | (turn == 3)
    return jnp.where(minus, -first, first), jnp.where((turn == 1) | (turn == 2), -second, second)


def wave_rows_call(couples, lon_count, wave_count):
    rows = 4 * couples.shape[0]
    block = rows // 4
    chunk = 32
    scale = 1.0 / math.sqrt(lon_count)

    def body(couples_ref, out):
        base = pl.program_id(0) * (block // 4)
        row = lax.broadcasted_iota(jnp.int32, (chunk, LANE), 0)
        lane = lax.broadcasted_iota(jnp.int32, (chunk, LANE), 1)

        def some_rows(index, carry):
            low = jnp.full((chunk, LANE), couples_ref[base + index * (chunk // 4)], jnp.int32)
            for n in range(1, chunk // 4):
                low = jnp.where(row // 4 == n, couples_ref[base + index * (chunk // 4) + n], low)
            wave = jnp.where(row // 2 % 2 == 0, low, wave_count - 1 - low)
            sine, cosine = sine_cosine(wave * lane, lon_count)
            s, c = sine_cosine(wave * LANE, lon_count)
            is_sine = row % 2 == 1
            a = jnp.where(is_sine, -sine, cosine) * scale
            b = jnp.where(is_sine, cosine, sine) * scale
            at = pl.ds(pl.multiple_of(index * chunk, chunk), chunk)
            for tile in range(lon_count // LANE):
                out[at, tile * LANE : (tile + 1) * LANE] = a.astype(BF)
                a, b = a * c - b * s, b * c + a * s
            return carry

        lax.fori_loop(0, block // chunk, some_rows, 0, unroll=2)

    return pl.pallas_call(
        body,
        name="wave_rows",
        grid_spec=pltpu.PrefetchScalarGridSpec(
            num_scalar_prefetch=1,
            grid=(rows // block,),
            in_specs=[],
            out_specs=pl.BlockSpec((block, lon_count), lambda i, *_: (i, 0)),
        ),
        out_shape=jax.ShapeDtypeStruct((rows, lon_count), BF),
    )(couples)


def fourier_call(place, here, waves, pieces, peers, cuts):
    parts = len(pieces)
    total_outs = peers * len(cuts)
    rows, lons = pieces[0].shape
    columns = waves.shape[0]
    block = columns // peers

    steps = 2
    share = columns // steps

    def body(place_ref, here_ref, w_ref, *refs):
        outs = refs[parts : parts + total_outs]
        whole, total = refs[parts + total_outs :]
        step = pl.program_id(0)

        @pl.when(step == 0)
        def _():
            for d in range(parts):
                start = jnp.bitwise_xor(place_ref[0], d) * lons
                whole[:, pl.ds(pl.multiple_of(start, LANE), lons)] = refs[d][...]

        total[pl.ds(pl.multiple_of(step * share, 32), share)] = lax.dot_general(
            w_ref[...], whole[...], (((1,), (1,)), ((), ())), preferred_element_type=F32
        ).astype(BF)

        @pl.when(step == steps - 1)
        def _():
            for number, (first, size) in enumerate(cuts):
                for e in range(peers):
                    start = jnp.bitwise_xor(here_ref[0], e) * block + first
                    outs[number * peers + e][...] = total[pl.ds(pl.multiple_of(start, 32), size)]

    return pl.pallas_call(
        body,
        name="fourier",
        grid_spec=pltpu.PrefetchScalarGridSpec(
            num_scalar_prefetch=2,
            grid=(steps,),
            in_specs=[pl.BlockSpec((share, parts * lons), lambda i, *_: (i, 0))]
            + [pl.BlockSpec((rows, lons), lambda i, *_: (0, 0))]
            + [pl.BlockSpec(memory_space=pltpu.VMEM)] * (parts - 1),
            out_specs=[
                pl.BlockSpec((size, rows), lambda i, *_: (0, 0)) for _, size in cuts for _ in range(peers)
            ],
            scratch_shapes=[pltpu.VMEM((rows, parts * lons), BF), pltpu.VMEM((columns, rows), BF)],
        ),
        out_shape=[
            jax.ShapeDtypeStruct((size, rows), BF) for _, size in cuts for _ in range(peers)
        ],
    )(place, here, waves, *in_vmem(pieces))


def by_slot(index, pairs, group):
    value = jnp.full(index.shape, pairs[group * GROUP], jnp.int32)
    for s in range(1, GROUP):
        value = jnp.where(index == s, pairs[group * GROUP + s], value)
    return value


def across(tiles, place):
    tiles = list(tiles)
    count = len(tiles)
    step = count // 2
    while step:
        shift = step * (LANE // count)
        upper = place // step % 2 == 1
        for d in range(count):
            if d // step % 2 == 0:
                low, high = tiles[d], tiles[d + step]
                tiles[d] = jnp.where(upper, pltpu.roll(high, shift, 1), low)
                tiles[d + step] = jnp.where(upper, high, pltpu.roll(low, LANE - shift, 1))
        step //= 2
    return tiles


def part_code(pairs, group, wave_count, half, par, lanes):
    lane = lax.broadcasted_iota(jnp.int32, (1, lanes), 1)
    slot = lane % GROUP
    r = 2 * (lane // GROUP + half) + par
    low = by_slot(slot, pairs, group)
    return 2 * slot + (r >= wave_count - low).astype(jnp.int32)


def forward_call(pairs, here, received, chunks, table, quadrature, first, groups):
    row_total, _, half_lat = table.shape
    wave_count = row_total - 1
    bands = len(received[0][1])
    shares = [block for _, blocks in received for block in in_vmem(blocks)]
    units = chunks[-1][1]
    row_block = GROUP * 4
    fields = LANE // SUB
    rows = fields * row_block
    per = wave_count // 2 * GROUP
    where_unit = {}
    for number, (lo, hi) in enumerate(chunks):
        for unit in range(lo, hi):
            where_unit[unit] = (number, unit - lo)

    def body(pairs_ref, here_ref, *refs):
        shared = refs[: len(shares)]
        table_ref, quad_ref, out, spread = refs[len(shares) : len(shares) + 4]
        recv = refs[len(shares) + 4 :]
        group = pl.program_id(0) + first
        for number in range(len(chunks)):
            start = group * row_block - received[number][0]
            mine = pl.ds(pl.multiple_of(start, row_block), row_block)
            for e in range(bands):
                band = jnp.bitwise_xor(here_ref[0], e)
                recv[number][band] = shared[number * bands + e][mine]
        lane = lax.broadcasted_iota(jnp.int32, (row_block, LANE), 1)
        place = lane // SUB
        turned = place * SUB + SUB - 1 - lane % SUB
        row = lax.broadcasted_iota(jnp.int32, (row_block, LANE), 0)
        low = by_slot(row // 4, pairs_ref, group)
        second = row // 2 % 2
        signs = [(1 - 2 * ((par + second * low) % 2)).astype(F32) for par in range(2)]

        def tile(band, unit):
            number, local = where_unit[unit]
            return recv[number][band, :, local * LANE : (local + 1) * LANE]

        for target in range(half_lat // LANE):
            at = slice(target * LANE, (target + 1) * LANE)
            north_tiles, south_tiles = [], []
            for d in range(fields):
                beta = fields * target + d
                band, unit = beta // units, beta % units
                north_tiles.append(tile(band, unit))
                south_tiles.append(tile(bands - 1 - band, units - 1 - unit))
            north_tiles, south_tiles = across(north_tiles, place), across(south_tiles, place)
            weight = quad_ref[0:1, at]
            for f in range(fields):
                north = north_tiles[f].astype(F32)
                south = jnp.take_along_axis(south_tiles[f].astype(F32), turned, axis=1)
                for par in range(2):
                    folded = (north + signs[par] * south) * weight
                    spread[par, f * row_block : (f + 1) * row_block, at] = folded.astype(BF)
        to = lax.broadcasted_iota(jnp.int32, (rows, rows), 0)
        source = lax.broadcasted_iota(jnp.int32, (rows, rows), 1)
        wanted = to // 2 % fields * row_block + to // (2 * fields) * 2 + to % 2
        order = (source == wanted).astype(BF)
        whole = table_ref[0:wave_count].reshape(wave_count // 2, 2, GROUP, half_lat)
        last = table_ref[wave_count]
        out[0, :, 2 * per :] = jnp.zeros((8, LANE), BF)
        for par in range(2):
            field = jnp.dot(order, spread[par], preferred_element_type=F32).astype(BF)
            matrix = whole[:, par].reshape(per, half_lat)
            product = lax.dot_general(
                field, matrix, (((1,), (1,)), ((), ())), preferred_element_type=F32
            )
            code = part_code(pairs_ref, group, wave_count, 0, par, per)
            kept = jnp.zeros((GROUP, per), F32)
            for b in range(2 * GROUP):
                kept = kept + jnp.where(code == b, product[b * 8 : (b + 1) * 8], 0.0)
            out[0, :, par * per : (par + 1) * per] = kept.astype(BF)
            if par == 0:
                ending = lax.dot_general(
                    field, last, (((1,), (1,)), ((), ())), preferred_element_type=F32
                )
                lane8 = lax.broadcasted_iota(jnp.int32, (1, GROUP), 1)
                kept = jnp.zeros((GROUP, GROUP), F32)
                for b in range(GROUP):
                    kept = kept + jnp.where(lane8 == b, ending[b * 16 + 8 : b * 16 + 16], 0.0)
                out[0, :, 2 * per : 2 * per + GROUP] = kept.astype(BF)

    return pl.pallas_call(
        body,
        name="forward",
        grid_spec=pltpu.PrefetchScalarGridSpec(
            num_scalar_prefetch=2,
            grid=(groups,),
            in_specs=[
                pl.BlockSpec(memory_space=pltpu.VMEM)
                if number % bands
                else pl.BlockSpec(block.shape, lambda g, *_: (0, 0))
                for number, block in enumerate(shares)
            ]
            + [
                pl.BlockSpec((row_total, GROUP, half_lat), lambda g, *_: (0, first + g, 0)),
                pl.BlockSpec((1, half_lat), lambda g, *_: (0, 0)),
            ],
            out_specs=pl.BlockSpec((1, 8, 2 * per + LANE), lambda g, *_: (g, 0, 0)),
            scratch_shapes=[pltpu.VMEM((2, rows, half_lat), BF)]
            + [pltpu.VMEM((bands, row_block, (hi - lo) * LANE), BF) for lo, hi in chunks],
        ),
        out_shape=jax.ShapeDtypeStruct((groups, 8, 2 * per + LANE), BF),
    )(pairs, here, *shares, table, quadrature)


def mix_matrix(operator, own):
    levels = operator.shape[0]
    n = levels * 4
    row = jnp.arange(n, dtype=jnp.int32)
    level = row // (4 * own) * own + row // 2 % own
    rest = row // (2 * own) % 2 * 2 + row % 2
    hot = (level[:, None] == jnp.arange(levels)[None, :]).astype(BF)
    spread = jnp.dot(jnp.dot(hot, operator, preferred_element_type=F32).astype(BF), hot.T,
                     preferred_element_type=F32)
    return jnp.where(rest[:, None] == rest[None, :], spread, 0.0).astype(BF), level


def inverse_call(pairs, place, gathered, project, rebuild, factors, table, first, before):
    row_total, slots, half_lat = table.shape
    wave_count = row_total - 1
    lev = len(gathered)
    groups, eight, lanes = gathered[0].shape
    n = lev * eight
    per = wave_count // 2 * GROUP
    rows = 2 * GROUP * eight
    own = eight // 4

    def body(pairs_ref, place_ref, *refs):
        got = refs[:lev]
        p_ref, r_ref, f_ref, table_ref = refs[lev : lev + 4]
        out, stack, x_ref = refs[-3:]
        group = pl.program_id(0) + first
        for d in range(lev):
            part = got[d][0 if d == 0 else pl.program_id(0)]
            stack[jnp.bitwise_xor(place_ref[0], d)] = part.astype(F32)
        lane = lax.broadcasted_iota(jnp.int32, (1, lanes), 1)
        place = lane // GROUP
        half = wave_count // 2
        r = jnp.where(
            place < half, 2 * place, jnp.where(place < 2 * half, 2 * (place - half) + 1, wave_count)
        )
        low = by_slot(lane % GROUP, pairs_ref, group)
        degree = jnp.where(r >= wave_count - low, r - 1, low + r).astype(F32)
        factor = degree * (degree + 1.0) / float(wave_count * wave_count)
        damping = 1.0 / (1.0 + factor * f_ref[:, 0:1])
        values = stack[...].reshape(n, lanes).astype(BF)
        modes = jnp.dot(p_ref[...], values, preferred_element_type=F32)
        damped = (modes * damping).astype(BF)
        x_ref[...] = jnp.dot(r_ref[...], damped, preferred_element_type=F32).astype(BF)
        whole = table_ref[0:wave_count].reshape(wave_count // 2, 2, GROUP, half_lat)
        sums = []
        for par in range(2):
            value = x_ref[:, par * per : (par + 1) * per].astype(F32)
            code = part_code(pairs_ref, group, wave_count, 0, par, per)
            spread = jnp.concatenate(
                [jnp.where(code == b, value, 0.0) for b in range(2 * GROUP)], axis=0
            ).astype(BF)
            matrix = whole[:, par].reshape(per, half_lat)
            sums.append(jnp.dot(spread, matrix, preferred_element_type=F32))
        tail = x_ref[:, 2 * per : 2 * per + GROUP].astype(F32)
        lane8 = lax.broadcasted_iota(jnp.int32, (1, GROUP), 1)
        nothing = jnp.zeros((eight, GROUP), F32)
        spread = jnp.concatenate(
            [
                jnp.where(lane8 == b // 2, tail, 0.0) if b % 2 else nothing
                for b in range(2 * GROUP)
            ],
            axis=0,
        ).astype(BF)
        sums[0] = sums[0] + jnp.dot(spread, table_ref[wave_count], preferred_element_type=F32)
        row = lax.broadcasted_iota(jnp.int32, (rows, LANE), 0)
        low = by_slot(row // (2 * eight), pairs_ref, group)
        sign = (1 - 2 * (row // eight % 2 * low % 2)).astype(F32)
        north = sums[0] + sums[1]
        back = LANE - 1 - lax.broadcasted_iota(jnp.int32, (rows, LANE), 1)
        tiles = half_lat // LANE
        for target in range(tiles):
            source = slice((tiles - 1 - target) * LANE, (tiles - target) * LANE)
            south = sign * (sums[0][:, source] - sums[1][:, source])
            south = jnp.take_along_axis(south, back, axis=1)
            upper = north[:, target * LANE : (target + 1) * LANE]
            for b in range(2 * GROUP):
                for f in range(2 * own):
                    at = slice(b * eight + 2 * f, b * eight + 2 * f + 2)
                    place = (f // own, f % own, b // 2, b % 2)
                    out[(*place, slice(None), slice(target * LANE, (target + 1) * LANE))] = upper[at]
                    out[
                        (
                            *place,
                            slice(None),
                            slice(half_lat + target * LANE, half_lat + (target + 1) * LANE),
                        )
                    ] = south[at]

    more = () if before is None else (before,)
    return pl.pallas_call(
        body,
        name="inverse",
        grid_spec=pltpu.PrefetchScalarGridSpec(
            num_scalar_prefetch=2,
            grid=(groups,),
            in_specs=[pl.BlockSpec((1, eight, lanes), lambda g, *_: (g, 0, 0))]
            + [pl.BlockSpec(memory_space=pltpu.VMEM)] * (lev - 1)
            + [
                pl.BlockSpec((n, n), lambda g, *_: (0, 0)),
                pl.BlockSpec((eight, n), lambda g, p, q: (q[0], 0)),
                pl.BlockSpec((n, LANE), lambda g, *_: (0, 0)),
                pl.BlockSpec((row_total, GROUP, half_lat), lambda g, *_: (0, first + g, 0)),
            ]
            + [pl.BlockSpec(memory_space=pl.ANY)] * len(more),
            out_specs=pl.BlockSpec(
                (2, own, GROUP, 2, 2, 2 * half_lat), lambda g, *_: (0, 0, first + g, 0, 0, 0)
            ),
            scratch_shapes=[
                pltpu.VMEM((lev, eight, lanes), F32),
                pltpu.VMEM((eight, lanes), BF),
            ],
        ),
        out_shape=jax.ShapeDtypeStruct((2, own, slots, 2, 2, 2 * half_lat), F32),
        input_output_aliases={lev + 6: 0} if more else {},
    )(pairs, place, *in_vmem(gathered), project, rebuild, factors, table, *more)


def in_vmem(arrays):
    return [arrays[0]] + [pltpu.with_memory_space_constraint(x, pltpu.VMEM) for x in arrays[1:]]


def swap(blocks, axis):
    count = len(blocks)
    return [blocks[0]] + [
        lax.ppermute(blocks[d], axis, [(i, i ^ d) for i in range(count)]) for d in range(1, count)
    ]


def tiled_local(u, v, t, operator, quadrature, table, couples, project, rebuild, factors):
    lev, lat = lax.axis_size("lev"), lax.axis_size("lat")
    levels, _, lons = u.shape
    own = levels // lev
    slots, row_total, _ = table.shape
    wave_count = row_total - 1
    place = lax.axis_index("lev").astype(jnp.int32)[None]
    here = lax.axis_index("lat").astype(jnp.int32)[None]
    flat = jnp.transpose(table, (1, 0, 2))
    received = []
    products = []
    for lo, hi in CHUNKS:
        products.append(products_call(place, u, v, t, operator, lev, lo, hi - lo))
    couples, products[-1] = lax.optimization_barrier((couples, products[-1]))
    waves = wave_rows_call(couples, lons * lev, wave_count)
    groups = slots // GROUP
    cut = -(-groups * CUT[0] // CUT[1])
    parts = ((0, cut), (cut, groups - cut))
    rows = 4 * GROUP
    for (lo, hi), blocks in zip(CHUNKS, products):
        blocks = swap(blocks, "lev")
        if lo > 0:
            blocks, late = lax.optimization_barrier((blocks, late))
        pieces = [x.reshape((hi - lo) * LANE, lons) for x in blocks]
        ending = hi == CHUNKS[-1][1]
        cuts = [(first * rows, count * rows) for first, count in parts]
        cuts = cuts if ending else [(0, groups * rows)]
        blocks = fourier_call(place, here, waves, pieces, lat, cuts)
        if lo == 0:
            blocks, late = lax.optimization_barrier(
                (blocks, (couples, quadrature, project, rebuild, factors))
            )
            late_couples, late_quadrature, project, rebuild, factors = late
            pairs = lax.dynamic_slice_in_dim(
                late_couples, lax.axis_index("lat") * slots, slots
            )
            to_modes, level = mix_matrix(project, own)
            to_levels, _ = mix_matrix(rebuild, own)
            factor_rows = jnp.broadcast_to(factors[level][:, None], (level.shape[0], LANE))
            late = (pairs, late_quadrature[None, :], to_modes, to_levels, factor_rows)
        shares = []
        for number, (first, _) in enumerate(cuts):
            shares.append((first, swap(blocks[number * lat : (number + 1) * lat], "lat")))
        received.append(shares)
    pairs, quadrature, to_modes, to_levels, factor_rows = late
    gathered = []
    for number, (first, count) in enumerate(parts):
        shares = [each[number if len(each) > 1 else 0] for each in received]
        block = forward_call(pairs, here, shares, CHUNKS, flat, quadrature, first, count)
        gathered.append(swap([block] * lev, "lev"))
    result = None
    for (first, _), blocks in zip(parts, gathered):
        result = inverse_call(
            pairs, place, blocks, to_modes, to_levels, factor_rows, flat, first, result
        )
    return result


def fits(lev, lat, band, lons, levels, slots, row_total, half_lat):
    return (
        lev % 2 == 0
        and lev & (lev - 1) == 0
        and lat & (lat - 1) == 0
        and lons * lev % 8 == 0
        and 2 * (row_total - 1) * LANE < 2**8 * lons * lev
        and levels == 2 * lev
        and band == CHUNKS[-1][1] * SUB
        and lons % LANE == 0
        and slots % GROUP == 0
        and row_total % 2 == 1
        and (row_total - 1) * GROUP % (2 * LANE) == 0
        and half_lat % LANE == 0
    )


def fourier_table(position_wavenumber_couples, lon_count, wave_count):
    repeated = jnp.repeat(position_wavenumber_couples, 4)
    column = jnp.arange(repeated.shape[0], dtype=jnp.int32)
    wavenumber = jnp.where(column // 2 % 2 == 0, repeated, wave_count - 1 - repeated)
    longitude = jnp.arange(lon_count, dtype=jnp.int32)
    phase_index = longitude[:, None] * wavenumber[None, :] % lon_count
    radians = phase_index.astype(jnp.float32) * (2.0 * math.pi / lon_count)
    values = jnp.where(column % 2 == 0, jnp.cos(radians), -jnp.sin(radians)) / math.sqrt(lon_count)
    return values.astype(jnp.bfloat16)


def row_layout(low_waves, wave_count, row_index):
    row_grid = row_index[None, :]
    low_grid = low_waves[:, None]
    boundary = wave_count - low_grid
    second_part = row_grid >= boundary
    parity = jnp.where(second_part, row_grid - boundary, row_grid) % 2
    degree = jnp.where(second_part, row_grid - 1, low_grid + row_grid)
    return (second_part, parity, degree)


def row_selector(second_part, parity):
    choices_two = jnp.arange(2, dtype=jnp.int32)
    parity_hit = parity[..., None] == choices_two
    part_hit = second_part.astype(jnp.int32)[..., None] == choices_two
    return parity_hit[..., :, None] & part_hit[..., None, :]


def damping(degree, eigen_backward_factors, wave_count):
    total = degree.astype(jnp.float32)
    factor = total * (total + 1.0) / float(wave_count * wave_count)
    return 1.0 / (1.0 + factor[:, :, None] * eigen_backward_factors[None, None, :])


def forward_legendre(
    by_wave, associated_polynomial_table, quadrature_factors_north, own_pairs, wave_count
):
    field_count, layer_tally, lat_count, column_count = by_wave.shape
    half_rows = lat_count // 2
    slot_count = column_count // 4
    northern = by_wave[:, :, :half_rows].astype(jnp.float32)
    southern = by_wave[:, :, half_rows:][:, :, ::-1].astype(jnp.float32)
    folded = (
        jnp.stack([northern + southern, northern - southern]) * quadrature_factors_north[:, None]
    )
    folded = folded.astype(jnp.bfloat16).reshape(
        2, field_count, layer_tally, half_rows, slot_count, 2, 2
    )
    folded = jnp.transpose(folded, (4, 3, 0, 5, 6, 1, 2)).reshape(slot_count, half_rows, -1)
    product = jnp.einsum(
        "srl,slc->src", associated_polynomial_table, folded, preferred_element_type=jnp.float32
    )
    product = product.reshape(slot_count, wave_count + 1, 2, 2, 2, field_count, layer_tally)
    layout = row_layout(own_pairs, wave_count, jnp.arange(wave_count + 1, dtype=jnp.int32))
    chosen = row_selector(layout[0], layout[1])
    return jnp.sum(jnp.where(chosen[..., None, None, None], product, 0.0), axis=(2, 3)).astype(
        jnp.bfloat16
    )


def inverse_legendre(implicit, associated_polynomial_table, own_pairs, wave_count):
    slot_count = implicit.shape[0]
    row_total = implicit.shape[1]
    field_count = implicit.shape[3]
    layer_tally = implicit.shape[4]
    layout = row_layout(own_pairs, wave_count, jnp.arange(row_total, dtype=jnp.int32))
    chosen = row_selector(layout[0], layout[1])
    spread = jnp.where(
        chosen[..., None, None, None], implicit[:, :, None, None], jnp.zeros((), implicit.dtype)
    )
    spread = spread.reshape(slot_count, row_total, -1)
    summed = jnp.einsum(
        "srl,src->slc", associated_polynomial_table, spread, preferred_element_type=jnp.float32
    )
    summed = summed.reshape(
        slot_count, associated_polynomial_table.shape[2], 2, 2, 2, field_count, layer_tally
    )
    northern = summed[:, :, 0] + summed[:, :, 1]
    southern = (summed[:, :, 0] - summed[:, :, 1])[:, ::-1]
    latitudes = jnp.concatenate([northern, southern], axis=1)
    return jnp.transpose(latitudes, (4, 5, 0, 2, 3, 1))


def plain_local(
    zonal_velocity,
    meridional_velocity,
    air_warmth,
    pressure_integration_operator,
    quadrature_factors_north,
    associated_polynomial_table,
    position_wavenumber_couples,
    layer_projection_operator,
    eigen_reconstruction_operator,
    eigen_backward_factors,
):
    layer_tally = air_warmth.shape[0]
    gravity_potential_surface = jnp.dot(
        pressure_integration_operator,
        air_warmth.reshape(layer_tally, -1),
        preferred_element_type=jnp.float32,
    )
    gravity_potential_surface = gravity_potential_surface.reshape(air_warmth.shape)
    eastward = zonal_velocity.astype(jnp.float32)
    northward = meridional_velocity.astype(jnp.float32)
    warmth_spectrum_field = air_warmth.astype(jnp.float32)
    products = jnp.stack(
        [
            eastward * northward + gravity_potential_surface,
            (eastward + northward) * warmth_spectrum_field,
        ]
    ).astype(jnp.bfloat16)
    by_level = lax.all_to_all(products, "lev", split_axis=1, concat_axis=3, tiled=True)
    field_count = by_level.shape[0]
    own_levels = by_level.shape[1]
    band_rows = by_level.shape[2]
    lon_count = by_level.shape[3]
    slot_count = associated_polynomial_table.shape[0]
    wave_count = associated_polynomial_table.shape[1] - 1
    row_total = wave_count + 1
    transform = fourier_table(position_wavenumber_couples, lon_count, wave_count)
    harmonic_coefficients_field = jnp.dot(
        by_level.reshape(-1, lon_count), transform, preferred_element_type=jnp.float32
    )
    harmonic_coefficients_field = harmonic_coefficients_field.astype(jnp.bfloat16).reshape(
        field_count, own_levels, band_rows, -1
    )
    by_wave = lax.all_to_all(
        harmonic_coefficients_field, "lat", split_axis=3, concat_axis=2, tiled=True
    )
    own_pairs = lax.dynamic_slice_in_dim(
        position_wavenumber_couples, lax.axis_index("lat") * slot_count, slot_count
    )
    spectral = forward_legendre(
        by_wave, associated_polynomial_table, quadrature_factors_north, own_pairs, wave_count
    )
    group_size = lax.axis_size("lev")
    padded_rows = -(-row_total // group_size) * group_size
    block_rows = padded_rows // group_size
    padded = jnp.pad(spectral, ((0, 0), (0, padded_rows - row_total), (0, 0), (0, 0), (0, 0)))
    received = lax.all_to_all(padded, "lev", split_axis=1, concat_axis=4, tiled=True)
    row_index = lax.axis_index("lev") * block_rows + jnp.arange(block_rows, dtype=jnp.int32)
    degree = row_layout(own_pairs, wave_count, row_index)[2]
    level_total = received.shape[4]
    flat_rows = received.reshape(-1, level_total)
    mode_values = jnp.dot(
        flat_rows, layer_projection_operator.T, preferred_element_type=jnp.float32
    ).reshape(received.shape)
    damped = (
        mode_values * damping(degree, eigen_backward_factors, wave_count)[:, :, None, None, :]
    ).astype(jnp.bfloat16)
    result = jnp.dot(
        damped.reshape(-1, level_total),
        eigen_reconstruction_operator.T,
        preferred_element_type=jnp.float32,
    )
    result = result.reshape(received.shape).astype(jnp.bfloat16)
    implicit = lax.all_to_all(result, "lev", split_axis=4, concat_axis=1, tiled=True)[:, :row_total]
    return inverse_legendre(implicit, associated_polynomial_table, own_pairs, wave_count)


def local(*args):
    table = args[5]
    sizes = args[0].shape
    if fits(
        lax.axis_size("lev"),
        lax.axis_size("lat"),
        sizes[1],
        sizes[2],
        sizes[0],
        table.shape[0],
        table.shape[1],
        table.shape[2],
    ):
        return tiled_local(*args)
    return plain_local(*args)


def solution(mesh):
    placed = (
        P(None, "lat", "lev"),
        P(None, "lat", "lev"),
        P(None, "lat", "lev"),
        P(),
        P(),
        P("lat", None, None),
        P(),
        P(),
        P(),
        P(),
    )
    return jax.shard_map(
        local,
        mesh=mesh,
        in_specs=placed,
        out_specs=P(None, "lev", "lat", None, None, None),
        check_vma=False,
    )
```

```python
import math

import jax
import jax.numpy as jnp
from jax import lax
from jax.experimental import pallas as pl
from jax.experimental.pallas import tpu as pltpu
from jax.sharding import PartitionSpec as P


BF = jnp.bfloat16
F32 = jnp.float32
LANE = 128
GROUP = 8
SUB = 32
CHUNKS = ((0, 2), (2, 5))
CUT = (1, 2)


def products_call(place, u, v, t, operator, lev, first, count):
    levels, _, lons = u.shape
    own = levels // lev
    split = SUB // 8

    def body(place_ref, op_ref, u_ref, v_ref, t_ref, *rest):
        outs, factors = rest[:lev], rest[lev]

        @pl.when(pl.program_id(0) == 0)
        def _():
            values = op_ref[...].astype(F32)
            for k in range(levels):
                for j in range(levels):
                    factors[k, j] = jnp.broadcast_to(values[k : k + 1, j : j + 1], (8, LANE))

        for tile in range(lons // LANE):
            at = slice(tile * LANE, (tile + 1) * LANE)
            warm = [t_ref[j, :, at].astype(F32).reshape(split, 8, LANE) for j in range(levels)]
            for d in range(lev):
                for own_level in range(own):
                    k = jnp.bitwise_xor(place_ref[0], d) * own + own_level
                    height = factors[k, 0] * warm[0]
                    for j in range(1, levels):
                        height = height + factors[k, j] * warm[j]
                    height = height.reshape(SUB, LANE)
                    east = u_ref[k, :, at].astype(F32)
                    north = v_ref[k, :, at].astype(F32)
                    here = t_ref[k, :, at].astype(F32)
                    outs[d][0, own_level, :, at] = (east * north + height).astype(BF)
                    outs[d][0, own + own_level, :, at] = ((east + north) * here).astype(BF)

    grid_in = pl.BlockSpec((levels, SUB, lons), lambda h, *_: (0, first + h, 0))
    return pl.pallas_call(
        body,
        name="products",
        grid_spec=pltpu.PrefetchScalarGridSpec(
            num_scalar_prefetch=1,
            grid=(count,),
            in_specs=[
                pl.BlockSpec((levels, levels), lambda h, *_: (0, 0)),
                grid_in,
                grid_in,
                grid_in,
            ],
            out_specs=[pl.BlockSpec((1, 2 * own, SUB, lons), lambda h, *_: (h, 0, 0, 0))] * lev,
            scratch_shapes=[pltpu.VMEM((levels, levels, 8, LANE), F32)],
        ),
        out_shape=[jax.ShapeDtypeStruct((count, 2 * own, SUB, lons), BF)] * lev,
    )(place, operator, u, v, t)


def whole_part(index, period):
    return ((index.astype(F32) + 0.5) * (1.0 / period)).astype(jnp.int32)


def sine_cosine(index, period):
    quarter = period // 4
    index = index - whole_part(index, period) * period
    turn = whole_part(index + period // 8, quarter)
    angle = (index - turn * quarter).astype(F32) * (2.0 * math.pi / period)
    square = angle * angle
    sine = 1.0 / 362880
    for c in (-1.0 / 5040, 1.0 / 120, -1.0 / 6, 1.0):
        sine = sine * square + c
    sine = sine * angle
    cosine = -1.0 / 3628800
    for c in (1.0 / 40320, -1.0 / 720, 1.0 / 24, -0.5, 1.0):
        cosine = cosine * square + c
    odd = (turn == 1) | (turn == 3)
    first = jnp.where(odd, cosine, sine)
    second = jnp.where(odd, sine, cosine)
    minus = (turn == 2) | (turn == 3)
    return jnp.where(minus, -first, first), jnp.where((turn == 1) | (turn == 2), -second, second)


def wave_rows_call(couples, lon_count, wave_count):
    rows = 4 * couples.shape[0]
    block = rows // 4
    chunk = 32
    scale = 1.0 / math.sqrt(lon_count)

    def body(couples_ref, out):
        base = pl.program_id(0) * (block // 4)
        row = lax.broadcasted_iota(jnp.int32, (chunk, LANE), 0)
        lane = lax.broadcasted_iota(jnp.int32, (chunk, LANE), 1)

        def some_rows(index, carry):
            low = jnp.full((chunk, LANE), couples_ref[base + index * (chunk // 4)], jnp.int32)
            for n in range(1, chunk // 4):
                low = jnp.where(row // 4 == n, couples_ref[base + index * (chunk // 4) + n], low)
            wave = jnp.where(row // 2 % 2 == 0, low, wave_count - 1 - low)
            sine, cosine = sine_cosine(wave * lane, lon_count)
            s, c = sine_cosine(wave * LANE, lon_count)
            is_sine = row % 2 == 1
            a = jnp.where(is_sine, -sine, cosine) * scale
            b = jnp.where(is_sine, cosine, sine) * scale
            at = pl.ds(pl.multiple_of(index * chunk, chunk), chunk)
            for tile in range(lon_count // LANE):
                out[at, tile * LANE : (tile + 1) * LANE] = a.astype(BF)
                a, b = a * c - b * s, b * c + a * s
            return carry

        lax.fori_loop(0, block // chunk, some_rows, 0, unroll=2)

    return pl.pallas_call(
        body,
        name="wave_rows",
        grid_spec=pltpu.PrefetchScalarGridSpec(
            num_scalar_prefetch=1,
            grid=(rows // block,),
            in_specs=[],
            out_specs=pl.BlockSpec((block, lon_count), lambda i, *_: (i, 0)),
        ),
        out_shape=jax.ShapeDtypeStruct((rows, lon_count), BF),
    )(couples)


def fourier_call(place, here, waves, pieces, peers, wanted):
    parts = len(pieces)
    total_outs = len(wanted)
    rows, lons = pieces[0].shape
    columns = waves.shape[0]
    block = columns // peers

    steps = 2
    share = columns // steps

    def body(place_ref, here_ref, w_ref, *refs):
        outs = refs[parts : parts + total_outs]
        whole, total = refs[parts + total_outs :]
        step = pl.program_id(0)

        @pl.when(step == 0)
        def _():
            for d in range(parts):
                start = jnp.bitwise_xor(place_ref[0], d) * lons
                whole[:, pl.ds(pl.multiple_of(start, LANE), lons)] = refs[d][...]

        total[pl.ds(pl.multiple_of(step * share, 32), share)] = lax.dot_general(
            w_ref[...], whole[...], (((1,), (1,)), ((), ())), preferred_element_type=F32
        ).astype(BF)

        @pl.when(step == steps - 1)
        def _():
            for out, (e, first, size) in zip(outs, wanted):
                start = jnp.bitwise_xor(here_ref[0], e) * block + first
                out[...] = total[pl.ds(pl.multiple_of(start, 32), size)]

    return pl.pallas_call(
        body,
        name="fourier",
        grid_spec=pltpu.PrefetchScalarGridSpec(
            num_scalar_prefetch=2,
            grid=(steps,),
            in_specs=[pl.BlockSpec((share, parts * lons), lambda i, *_: (i, 0))]
            + [pl.BlockSpec((rows, lons), lambda i, *_: (0, 0))]
            + [pl.BlockSpec(memory_space=pltpu.VMEM)] * (parts - 1),
            out_specs=[pl.BlockSpec((size, rows), lambda i, *_: (0, 0)) for _, _, size in wanted],
            scratch_shapes=[pltpu.VMEM((rows, parts * lons), BF), pltpu.VMEM((columns, rows), BF)],
        ),
        out_shape=[jax.ShapeDtypeStruct((size, rows), BF) for _, _, size in wanted],
    )(place, here, waves, *in_vmem(pieces))


def by_slot(index, pairs, group):
    value = jnp.full(index.shape, pairs[group * GROUP], jnp.int32)
    for s in range(1, GROUP):
        value = jnp.where(index == s, pairs[group * GROUP + s], value)
    return value


def across(tiles, place):
    tiles = list(tiles)
    count = len(tiles)
    step = count // 2
    while step:
        shift = step * (LANE // count)
        upper = place // step % 2 == 1
        for d in range(count):
            if d // step % 2 == 0:
                low, high = tiles[d], tiles[d + step]
                tiles[d] = jnp.where(upper, pltpu.roll(high, shift, 1), low)
                tiles[d + step] = jnp.where(upper, high, pltpu.roll(low, LANE - shift, 1))
        step //= 2
    return tiles


def part_code(pairs, group, wave_count, half, par, lanes):
    lane = lax.broadcasted_iota(jnp.int32, (1, lanes), 1)
    slot = lane % GROUP
    r = 2 * (lane // GROUP + half) + par
    low = by_slot(slot, pairs, group)
    return 2 * slot + (r >= wave_count - low).astype(jnp.int32)


def forward_call(pairs, here, received, chunks, table, quadrature, first, groups):
    row_total, _, half_lat = table.shape
    wave_count = row_total - 1
    bands = len(received[0])
    begins = [[begin for begin, _ in parts] for parts in received]
    shares = [block for parts in received for block in in_vmem([block for _, block in parts])]
    units = chunks[-1][1]
    row_block = GROUP * 4
    fields = LANE // SUB
    rows = fields * row_block
    per = wave_count // 2 * GROUP
    where_unit = {}
    for number, (lo, hi) in enumerate(chunks):
        for unit in range(lo, hi):
            where_unit[unit] = (number, unit - lo)

    def body(pairs_ref, here_ref, *refs):
        shared = refs[: len(shares)]
        table_ref, quad_ref, out, spread = refs[len(shares) : len(shares) + 4]
        recv = refs[len(shares) + 4 :]
        group = pl.program_id(0) + first
        for number in range(len(chunks)):
            for e in range(bands):
                start = group * row_block - begins[number][e]
                mine = pl.ds(pl.multiple_of(start, row_block), row_block)
                band = jnp.bitwise_xor(here_ref[0], e)
                recv[number][band] = shared[number * bands + e][mine]
        lane = lax.broadcasted_iota(jnp.int32, (row_block, LANE), 1)
        place = lane // SUB
        turned = place * SUB + SUB - 1 - lane % SUB
        row = lax.broadcasted_iota(jnp.int32, (row_block, LANE), 0)
        low = by_slot(row // 4, pairs_ref, group)
        second = row // 2 % 2
        signs = [(1 - 2 * ((par + second * low) % 2)).astype(F32) for par in range(2)]

        def tile(band, unit):
            number, local = where_unit[unit]
            return recv[number][band, :, local * LANE : (local + 1) * LANE]

        for target in range(half_lat // LANE):
            at = slice(target * LANE, (target + 1) * LANE)
            north_tiles, south_tiles = [], []
            for d in range(fields):
                beta = fields * target + d
                band, unit = beta // units, beta % units
                north_tiles.append(tile(band, unit))
                south_tiles.append(tile(bands - 1 - band, units - 1 - unit))
            north_tiles, south_tiles = across(north_tiles, place), across(south_tiles, place)
            weight = quad_ref[0:1, at]
            for f in range(fields):
                north = north_tiles[f].astype(F32)
                south = jnp.take_along_axis(south_tiles[f].astype(F32), turned, axis=1)
                for par in range(2):
                    folded = (north + signs[par] * south) * weight
                    spread[par, f * row_block : (f + 1) * row_block, at] = folded.astype(BF)
        to = lax.broadcasted_iota(jnp.int32, (rows, rows), 0)
        source = lax.broadcasted_iota(jnp.int32, (rows, rows), 1)
        wanted = to // 2 % fields * row_block + to // (2 * fields) * 2 + to % 2
        order = (source == wanted).astype(BF)
        whole = table_ref[0:wave_count].reshape(wave_count // 2, 2, GROUP, half_lat)
        last = table_ref[wave_count]
        out[0, :, 2 * per :] = jnp.zeros((8, LANE), BF)
        for par in range(2):
            field = jnp.dot(order, spread[par], preferred_element_type=F32).astype(BF)
            matrix = whole[:, par].reshape(per, half_lat)
            product = lax.dot_general(
                field, matrix, (((1,), (1,)), ((), ())), preferred_element_type=F32
            )
            code = part_code(pairs_ref, group, wave_count, 0, par, per)
            kept = jnp.zeros((GROUP, per), F32)
            for b in range(2 * GROUP):
                kept = kept + jnp.where(code == b, product[b * 8 : (b + 1) * 8], 0.0)
            out[0, :, par * per : (par + 1) * per] = kept.astype(BF)
            if par == 0:
                ending = lax.dot_general(
                    field, last, (((1,), (1,)), ((), ())), preferred_element_type=F32
                )
                lane8 = lax.broadcasted_iota(jnp.int32, (1, GROUP), 1)
                kept = jnp.zeros((GROUP, GROUP), F32)
                for b in range(GROUP):
                    kept = kept + jnp.where(lane8 == b, ending[b * 16 + 8 : b * 16 + 16], 0.0)
                out[0, :, 2 * per : 2 * per + GROUP] = kept.astype(BF)

    return pl.pallas_call(
        body,
        name="forward",
        grid_spec=pltpu.PrefetchScalarGridSpec(
            num_scalar_prefetch=2,
            grid=(groups,),
            in_specs=[
                pl.BlockSpec(memory_space=pltpu.VMEM)
                if number % bands
                else pl.BlockSpec(block.shape, lambda g, *_: (0, 0))
                for number, block in enumerate(shares)
            ]
            + [
                pl.BlockSpec((row_total, GROUP, half_lat), lambda g, *_: (0, first + g, 0)),
                pl.BlockSpec((1, half_lat), lambda g, *_: (0, 0)),
            ],
            out_specs=pl.BlockSpec((1, 8, 2 * per + LANE), lambda g, *_: (g, 0, 0)),
            scratch_shapes=[pltpu.VMEM((2, rows, half_lat), BF)]
            + [pltpu.VMEM((bands, row_block, (hi - lo) * LANE), BF) for lo, hi in chunks],
        ),
        out_shape=jax.ShapeDtypeStruct((groups, 8, 2 * per + LANE), BF),
    )(pairs, here, *shares, table, quadrature)


def mix_matrix(operator, own):
    levels = operator.shape[0]
    n = levels * 4
    row = jnp.arange(n, dtype=jnp.int32)
    level = row // (4 * own) * own + row // 2 % own
    rest = row // (2 * own) % 2 * 2 + row % 2
    hot = (level[:, None] == jnp.arange(levels)[None, :]).astype(BF)
    spread = jnp.dot(jnp.dot(hot, operator, preferred_element_type=F32).astype(BF), hot.T,
                     preferred_element_type=F32)
    return jnp.where(rest[:, None] == rest[None, :], spread, 0.0).astype(BF)


def inverse_call(pairs, place, gathered, project, rebuild, factors, table, first, before):
    row_total, slots, half_lat = table.shape
    wave_count = row_total - 1
    lev = len(gathered)
    groups, eight, lanes = gathered[0].shape
    n = lev * eight
    per = wave_count // 2 * GROUP
    rows = 2 * GROUP * eight
    own = eight // 4

    def body(pairs_ref, place_ref, *refs):
        got = refs[:lev]
        p_ref, r_ref, f_ref, table_ref = refs[lev : lev + 4]
        out, stack, damping, x_ref = refs[-4:]
        group = pl.program_id(0) + first
        for d in range(lev):
            part = got[d][0 if d == 0 else pl.program_id(0)]
            stack[jnp.bitwise_xor(place_ref[0], d)] = part
        lane = lax.broadcasted_iota(jnp.int32, (1, lanes), 1)
        place = lane // GROUP
        half = wave_count // 2
        r = jnp.where(
            place < half, 2 * place, jnp.where(place < 2 * half, 2 * (place - half) + 1, wave_count)
        )
        low = by_slot(lane % GROUP, pairs_ref, group)
        second = r >= wave_count - low
        codes = 2 * (lane % GROUP) + second.astype(jnp.int32)
        degree = jnp.where(second, r - 1, low + r).astype(F32)
        factor = degree * (degree + 1.0) / float(wave_count * wave_count)
        levels = lev * own
        level = lax.broadcasted_iota(jnp.int32, (levels, 1), 0)
        coefficient = jnp.full((levels, 1), f_ref[0], F32)
        for q in range(1, levels):
            coefficient = jnp.where(level == q, f_ref[q], coefficient)
        damping[...] = 1.0 / (1.0 + factor * coefficient)
        values = stack[...].reshape(n, lanes)
        modes = jnp.dot(p_ref[...], values, preferred_element_type=F32)
        own_level = lax.broadcasted_iota(jnp.int32, (eight, 1), 0) // 2 % own
        damped = []
        for owner in range(lev):
            rate = damping[owner * own : owner * own + 1]
            for q in range(1, own):
                rate = jnp.where(own_level == q, damping[owner * own + q : owner * own + q + 1], rate)
            damped.append(modes[owner * eight : (owner + 1) * eight] * rate)
        damped = jnp.concatenate(damped, axis=0).astype(BF)
        x_ref[...] = jnp.dot(r_ref[...], damped, preferred_element_type=F32).astype(BF)
        whole = table_ref[0:wave_count].reshape(wave_count // 2, 2, GROUP, half_lat)
        sums = []
        for par in range(2):
            value = x_ref[:, par * per : (par + 1) * per].astype(F32)
            code = codes[:, par * per : (par + 1) * per]
            spread = jnp.concatenate(
                [jnp.where(code == b, value, 0.0) for b in range(2 * GROUP)], axis=0
            ).astype(BF)
            matrix = whole[:, par].reshape(per, half_lat)
            sums.append(jnp.dot(spread, matrix, preferred_element_type=F32))
        tail = x_ref[:, 2 * per : 2 * per + GROUP].astype(F32)
        lane8 = lax.broadcasted_iota(jnp.int32, (1, GROUP), 1)
        nothing = jnp.zeros((eight, GROUP), F32)
        spread = jnp.concatenate(
            [
                jnp.where(lane8 == b // 2, tail, 0.0) if b % 2 else nothing
                for b in range(2 * GROUP)
            ],
            axis=0,
        ).astype(BF)
        sums[0] = sums[0] + jnp.dot(spread, table_ref[wave_count], preferred_element_type=F32)
        row = lax.broadcasted_iota(jnp.int32, (rows, LANE), 0)
        low = by_slot(row // (2 * eight), pairs_ref, group)
        sign = (1 - 2 * (row // eight % 2 * low % 2)).astype(F32)
        north = sums[0] + sums[1]
        back = LANE - 1 - lax.broadcasted_iota(jnp.int32, (rows, LANE), 1)
        tiles = half_lat // LANE
        for target in range(tiles):
            source = slice((tiles - 1 - target) * LANE, (tiles - target) * LANE)
            south = sign * (sums[0][:, source] - sums[1][:, source])
            south = jnp.take_along_axis(south, back, axis=1)
            upper = north[:, target * LANE : (target + 1) * LANE]
            for b in range(2 * GROUP):
                for f in range(2 * own):
                    at = slice(b * eight + 2 * f, b * eight + 2 * f + 2)
                    place = (f // own, f % own, b // 2, b % 2)
                    out[(*place, slice(None), slice(target * LANE, (target + 1) * LANE))] = upper[at]
                    out[
                        (
                            *place,
                            slice(None),
                            slice(half_lat + target * LANE, half_lat + (target + 1) * LANE),
                        )
                    ] = south[at]

    more = () if before is None else (before,)
    return pl.pallas_call(
        body,
        name="inverse",
        grid_spec=pltpu.PrefetchScalarGridSpec(
            num_scalar_prefetch=2,
            grid=(groups,),
            in_specs=[pl.BlockSpec((1, eight, lanes), lambda g, *_: (g, 0, 0))]
            + [pl.BlockSpec(memory_space=pltpu.VMEM)] * (lev - 1)
            + [
                pl.BlockSpec((n, n), lambda g, *_: (0, 0)),
                pl.BlockSpec((eight, n), lambda g, p, q: (q[0], 0)),
                pl.BlockSpec(memory_space=pltpu.SMEM),
                pl.BlockSpec((row_total, GROUP, half_lat), lambda g, *_: (0, first + g, 0)),
            ]
            + [pl.BlockSpec(memory_space=pl.ANY)] * len(more),
            out_specs=pl.BlockSpec(
                (2, own, GROUP, 2, 2, 2 * half_lat), lambda g, *_: (0, 0, first + g, 0, 0, 0)
            ),
            scratch_shapes=[
                pltpu.VMEM((lev, eight, lanes), BF),
                pltpu.VMEM((lev * own, lanes), F32),
                pltpu.VMEM((eight, lanes), BF),
            ],
        ),
        out_shape=jax.ShapeDtypeStruct((2, own, slots, 2, 2, 2 * half_lat), F32),
        input_output_aliases={lev + 6: 0} if more else {},
    )(pairs, place, *in_vmem(gathered), project, rebuild, factors, table, *more)


def in_vmem(arrays):
    return [arrays[0]] + [pltpu.with_memory_space_constraint(x, pltpu.VMEM) for x in arrays[1:]]


def send(block, axis, bits):
    if bits == 0:
        return block
    return lax.ppermute(block, axis, [(i, i ^ bits) for i in range(lax.axis_size(axis))])


def swap(blocks, axis):
    return [send(block, axis, d) for d, block in enumerate(blocks)]


def tiled_local(u, v, t, operator, quadrature, table, couples, project, rebuild, factors):
    lev, lat = lax.axis_size("lev"), lax.axis_size("lat")
    levels, _, lons = u.shape
    own = levels // lev
    slots, row_total, _ = table.shape
    wave_count = row_total - 1
    place = lax.axis_index("lev").astype(jnp.int32)[None]
    here = lax.axis_index("lat").astype(jnp.int32)[None]
    flat = jnp.transpose(table, (1, 0, 2))
    received = []
    products = []
    for lo, hi in CHUNKS:
        products.append(products_call(place, u, v, t, operator, lev, lo, hi - lo))
    couples, products[-1] = lax.optimization_barrier((couples, products[-1]))
    waves = wave_rows_call(couples, lons * lev, wave_count)
    groups = slots // GROUP
    cut = -(-groups * CUT[0] // CUT[1])
    parts = ((0, cut), (cut, groups - cut))
    rows = 4 * GROUP
    for (lo, hi), blocks in zip(CHUNKS, products):
        blocks = swap(blocks, "lev")
        if lo > 0:
            blocks, late = lax.optimization_barrier((blocks, late))
        pieces = [x.reshape((hi - lo) * LANE, lons) for x in blocks]
        ending = hi == CHUNKS[-1][1]
        near = lat // 2 if ending else lat
        wanted = [(e, 0, groups * rows) for e in range(near)]
        for first, count in parts if ending else ():
            wanted += [(e, first * rows, count * rows) for e in range(near, lat)]
        blocks = fourier_call(place, here, waves, pieces, lat, wanted)
        if lo == 0:
            blocks, late = lax.optimization_barrier(
                (blocks, (couples, quadrature, project, rebuild))
            )
            late_couples, late_quadrature, project, rebuild = late
            pairs = lax.dynamic_slice_in_dim(
                late_couples, lax.axis_index("lat") * slots, slots
            )
            to_modes = mix_matrix(project, own)
            to_levels = mix_matrix(rebuild, own)
            late = (pairs, late_quadrature[None, :], to_modes, to_levels)
        whole = [(0, send(blocks[e], "lat", e)) for e in range(near)]
        shares = []
        for number in range(len(parts) if ending else 1):
            at = slice(near + number * (lat - near), near + (number + 1) * (lat - near))
            rest = [
                (first, send(block, "lat", e))
                for block, (e, first, _) in zip(blocks[at], wanted[at])
            ]
            shares.append(whole + rest)
        received.append(shares)
    pairs, quadrature, to_modes, to_levels = late
    gathered = []
    for number, (first, count) in enumerate(parts):
        shares = [each[number if len(each) > 1 else 0] for each in received]
        block = forward_call(pairs, here, shares, CHUNKS, flat, quadrature, first, count)
        gathered.append(swap([block] * lev, "lev"))
    result = None
    for (first, _), blocks in zip(parts, gathered):
        result = inverse_call(
            pairs, place, blocks, to_modes, to_levels, factors, flat, first, result
        )
    return result


def fits(lev, lat, band, lons, levels, slots, row_total, half_lat):
    return (
        lev % 2 == 0
        and lev & (lev - 1) == 0
        and lat & (lat - 1) == 0
        and lons * lev % 8 == 0
        and 2 * (row_total - 1) * LANE < 2**8 * lons * lev
        and levels == 2 * lev
        and band == CHUNKS[-1][1] * SUB
        and lons % LANE == 0
        and slots % GROUP == 0
        and row_total % 2 == 1
        and (row_total - 1) * GROUP % (2 * LANE) == 0
        and half_lat % LANE == 0
    )


def fourier_table(position_wavenumber_couples, lon_count, wave_count):
    repeated = jnp.repeat(position_wavenumber_couples, 4)
    column = jnp.arange(repeated.shape[0], dtype=jnp.int32)
    wavenumber = jnp.where(column // 2 % 2 == 0, repeated, wave_count - 1 - repeated)
    longitude = jnp.arange(lon_count, dtype=jnp.int32)
    phase_index = longitude[:, None] * wavenumber[None, :] % lon_count
    radians = phase_index.astype(jnp.float32) * (2.0 * math.pi / lon_count)
    values = jnp.where(column % 2 == 0, jnp.cos(radians), -jnp.sin(radians)) / math.sqrt(lon_count)
    return values.astype(jnp.bfloat16)


def row_layout(low_waves, wave_count, row_index):
    row_grid = row_index[None, :]
    low_grid = low_waves[:, None]
    boundary = wave_count - low_grid
    second_part = row_grid >= boundary
    parity = jnp.where(second_part, row_grid - boundary, row_grid) % 2
    degree = jnp.where(second_part, row_grid - 1, low_grid + row_grid)
    return (second_part, parity, degree)


def row_selector(second_part, parity):
    choices_two = jnp.arange(2, dtype=jnp.int32)
    parity_hit = parity[..., None] == choices_two
    part_hit = second_part.astype(jnp.int32)[..., None] == choices_two
    return parity_hit[..., :, None] & part_hit[..., None, :]


def damping(degree, eigen_backward_factors, wave_count):
    total = degree.astype(jnp.float32)
    factor = total * (total + 1.0) / float(wave_count * wave_count)
    return 1.0 / (1.0 + factor[:, :, None] * eigen_backward_factors[None, None, :])


def forward_legendre(
    by_wave, associated_polynomial_table, quadrature_factors_north, own_pairs, wave_count
):
    field_count, layer_tally, lat_count, column_count = by_wave.shape
    half_rows = lat_count // 2
    slot_count = column_count // 4
    northern = by_wave[:, :, :half_rows].astype(jnp.float32)
    southern = by_wave[:, :, half_rows:][:, :, ::-1].astype(jnp.float32)
    folded = (
        jnp.stack([northern + southern, northern - southern]) * quadrature_factors_north[:, None]
    )
    folded = folded.astype(jnp.bfloat16).reshape(
        2, field_count, layer_tally, half_rows, slot_count, 2, 2
    )
    folded = jnp.transpose(folded, (4, 3, 0, 5, 6, 1, 2)).reshape(slot_count, half_rows, -1)
    product = jnp.einsum(
        "srl,slc->src", associated_polynomial_table, folded, preferred_element_type=jnp.float32
    )
    product = product.reshape(slot_count, wave_count + 1, 2, 2, 2, field_count, layer_tally)
    layout = row_layout(own_pairs, wave_count, jnp.arange(wave_count + 1, dtype=jnp.int32))
    chosen = row_selector(layout[0], layout[1])
    return jnp.sum(jnp.where(chosen[..., None, None, None], product, 0.0), axis=(2, 3)).astype(
        jnp.bfloat16
    )


def inverse_legendre(implicit, associated_polynomial_table, own_pairs, wave_count):
    slot_count = implicit.shape[0]
    row_total = implicit.shape[1]
    field_count = implicit.shape[3]
    layer_tally = implicit.shape[4]
    layout = row_layout(own_pairs, wave_count, jnp.arange(row_total, dtype=jnp.int32))
    chosen = row_selector(layout[0], layout[1])
    spread = jnp.where(
        chosen[..., None, None, None], implicit[:, :, None, None], jnp.zeros((), implicit.dtype)
    )
    spread = spread.reshape(slot_count, row_total, -1)
    summed = jnp.einsum(
        "srl,src->slc", associated_polynomial_table, spread, preferred_element_type=jnp.float32
    )
    summed = summed.reshape(
        slot_count, associated_polynomial_table.shape[2], 2, 2, 2, field_count, layer_tally
    )
    northern = summed[:, :, 0] + summed[:, :, 1]
    southern = (summed[:, :, 0] - summed[:, :, 1])[:, ::-1]
    latitudes = jnp.concatenate([northern, southern], axis=1)
    return jnp.transpose(latitudes, (4, 5, 0, 2, 3, 1))


def plain_local(
    zonal_velocity,
    meridional_velocity,
    air_warmth,
    pressure_integration_operator,
    quadrature_factors_north,
    associated_polynomial_table,
    position_wavenumber_couples,
    layer_projection_operator,
    eigen_reconstruction_operator,
    eigen_backward_factors,
):
    layer_tally = air_warmth.shape[0]
    gravity_potential_surface = jnp.dot(
        pressure_integration_operator,
        air_warmth.reshape(layer_tally, -1),
        preferred_element_type=jnp.float32,
    )
    gravity_potential_surface = gravity_potential_surface.reshape(air_warmth.shape)
    eastward = zonal_velocity.astype(jnp.float32)
    northward = meridional_velocity.astype(jnp.float32)
    warmth_spectrum_field = air_warmth.astype(jnp.float32)
    products = jnp.stack(
        [
            eastward * northward + gravity_potential_surface,
            (eastward + northward) * warmth_spectrum_field,
        ]
    ).astype(jnp.bfloat16)
    by_level = lax.all_to_all(products, "lev", split_axis=1, concat_axis=3, tiled=True)
    field_count = by_level.shape[0]
    own_levels = by_level.shape[1]
    band_rows = by_level.shape[2]
    lon_count = by_level.shape[3]
    slot_count = associated_polynomial_table.shape[0]
    wave_count = associated_polynomial_table.shape[1] - 1
    row_total = wave_count + 1
    transform = fourier_table(position_wavenumber_couples, lon_count, wave_count)
    harmonic_coefficients_field = jnp.dot(
        by_level.reshape(-1, lon_count), transform, preferred_element_type=jnp.float32
    )
    harmonic_coefficients_field = harmonic_coefficients_field.astype(jnp.bfloat16).reshape(
        field_count, own_levels, band_rows, -1
    )
    by_wave = lax.all_to_all(
        harmonic_coefficients_field, "lat", split_axis=3, concat_axis=2, tiled=True
    )
    own_pairs = lax.dynamic_slice_in_dim(
        position_wavenumber_couples, lax.axis_index("lat") * slot_count, slot_count
    )
    spectral = forward_legendre(
        by_wave, associated_polynomial_table, quadrature_factors_north, own_pairs, wave_count
    )
    group_size = lax.axis_size("lev")
    padded_rows = -(-row_total // group_size) * group_size
    block_rows = padded_rows // group_size
    padded = jnp.pad(spectral, ((0, 0), (0, padded_rows - row_total), (0, 0), (0, 0), (0, 0)))
    received = lax.all_to_all(padded, "lev", split_axis=1, concat_axis=4, tiled=True)
    row_index = lax.axis_index("lev") * block_rows + jnp.arange(block_rows, dtype=jnp.int32)
    degree = row_layout(own_pairs, wave_count, row_index)[2]
    level_total = received.shape[4]
    flat_rows = received.reshape(-1, level_total)
    mode_values = jnp.dot(
        flat_rows, layer_projection_operator.T, preferred_element_type=jnp.float32
    ).reshape(received.shape)
    damped = (
        mode_values * damping(degree, eigen_backward_factors, wave_count)[:, :, None, None, :]
    ).astype(jnp.bfloat16)
    result = jnp.dot(
        damped.reshape(-1, level_total),
        eigen_reconstruction_operator.T,
        preferred_element_type=jnp.float32,
    )
    result = result.reshape(received.shape).astype(jnp.bfloat16)
    implicit = lax.all_to_all(result, "lev", split_axis=4, concat_axis=1, tiled=True)[:, :row_total]
    return inverse_legendre(implicit, associated_polynomial_table, own_pairs, wave_count)


def local(*args):
    table = args[5]
    sizes = args[0].shape
    if fits(
        lax.axis_size("lev"),
        lax.axis_size("lat"),
        sizes[1],
        sizes[2],
        sizes[0],
        table.shape[0],
        table.shape[1],
        table.shape[2],
    ):
        return tiled_local(*args)
    return plain_local(*args)


def solution(mesh):
    placed = (
        P(None, "lat", "lev"),
        P(None, "lat", "lev"),
        P(None, "lat", "lev"),
        P(),
        P(),
        P("lat", None, None),
        P(),
        P(),
        P(),
        P(),
    )
    return jax.shard_map(
        local,
        mesh=mesh,
        in_specs=placed,
        out_specs=P(None, "lev", "lat", None, None, None),
        check_vma=False,
    )
```

```python
import math

import jax
import jax.numpy as jnp
from jax import lax
from jax.experimental import pallas as pl
from jax.experimental.pallas import tpu as pltpu
from jax.sharding import PartitionSpec as P


BF = jnp.bfloat16
F32 = jnp.float32
LANE = 128
GROUP = 8
SUB = 32
CHUNKS = ((0, 2), (2, 5))
CUT = (1, 2)


def products_call(place, u, v, t, operator, lev, first, count):
    levels, _, lons = u.shape
    own = levels // lev
    split = SUB // 8

    def body(place_ref, op_ref, u_ref, v_ref, t_ref, *rest):
        outs, factors = rest[:lev], rest[lev]

        @pl.when(pl.program_id(0) == 0)
        def _():
            values = op_ref[...].astype(F32)
            for k in range(levels):
                for j in range(levels):
                    factors[k, j] = jnp.broadcast_to(values[k : k + 1, j : j + 1], (8, LANE))

        for tile in range(lons // LANE):
            at = slice(tile * LANE, (tile + 1) * LANE)
            warm = [t_ref[j, :, at].astype(F32).reshape(split, 8, LANE) for j in range(levels)]
            for d in range(lev):
                for own_level in range(own):
                    k = jnp.bitwise_xor(place_ref[0], d) * own + own_level
                    height = factors[k, 0] * warm[0]
                    for j in range(1, levels):
                        height = height + factors[k, j] * warm[j]
                    height = height.reshape(SUB, LANE)
                    east = u_ref[k, :, at].astype(F32)
                    north = v_ref[k, :, at].astype(F32)
                    here = t_ref[k, :, at].astype(F32)
                    outs[d][0, own_level, :, at] = (east * north + height).astype(BF)
                    outs[d][0, own + own_level, :, at] = ((east + north) * here).astype(BF)

    grid_in = pl.BlockSpec((levels, SUB, lons), lambda h, *_: (0, first + h, 0))
    return pl.pallas_call(
        body,
        name="products",
        grid_spec=pltpu.PrefetchScalarGridSpec(
            num_scalar_prefetch=1,
            grid=(count,),
            in_specs=[
                pl.BlockSpec((levels, levels), lambda h, *_: (0, 0)),
                grid_in,
                grid_in,
                grid_in,
            ],
            out_specs=[pl.BlockSpec((1, 2 * own, SUB, lons), lambda h, *_: (h, 0, 0, 0))] * lev,
            scratch_shapes=[pltpu.VMEM((levels, levels, 8, LANE), F32)],
        ),
        out_shape=[jax.ShapeDtypeStruct((count, 2 * own, SUB, lons), BF)] * lev,
    )(place, operator, u, v, t)


def whole_part(index, period):
    return ((index.astype(F32) + 0.5) * (1.0 / period)).astype(jnp.int32)


def sine_cosine(index, period):
    quarter = period // 4
    index = index - whole_part(index, period) * period
    turn = whole_part(index + period // 8, quarter)
    angle = (index - turn * quarter).astype(F32) * (2.0 * math.pi / period)
    square = angle * angle
    sine = 1.0 / 362880
    for c in (-1.0 / 5040, 1.0 / 120, -1.0 / 6, 1.0):
        sine = sine * square + c
    sine = sine * angle
    cosine = -1.0 / 3628800
    for c in (1.0 / 40320, -1.0 / 720, 1.0 / 24, -0.5, 1.0):
        cosine = cosine * square + c
    odd = (turn == 1) | (turn == 3)
    first = jnp.where(odd, cosine, sine)
    second = jnp.where(odd, sine, cosine)
    minus = (turn == 2) | (turn == 3)
    return jnp.where(minus, -first, first), jnp.where((turn == 1) | (turn == 2), -second, second)


def wave_rows_call(couples, lon_count, wave_count):
    rows = 4 * couples.shape[0]
    block = rows // 4
    chunk = 32
    scale = 1.0 / math.sqrt(lon_count)

    def body(couples_ref, out):
        base = pl.program_id(0) * (block // 4)
        row = lax.broadcasted_iota(jnp.int32, (chunk, LANE), 0)
        lane = lax.broadcasted_iota(jnp.int32, (chunk, LANE), 1)

        def some_rows(index, carry):
            low = jnp.full((chunk, LANE), couples_ref[base + index * (chunk // 4)], jnp.int32)
            for n in range(1, chunk // 4):
                low = jnp.where(row // 4 == n, couples_ref[base + index * (chunk // 4) + n], low)
            wave = jnp.where(row // 2 % 2 == 0, low, wave_count - 1 - low)
            sine, cosine = sine_cosine(wave * lane, lon_count)
            s, c = sine_cosine(wave * LANE, lon_count)
            is_sine = row % 2 == 1
            a = jnp.where(is_sine, -sine, cosine) * scale
            b = jnp.where(is_sine, cosine, sine) * scale
            at = pl.ds(pl.multiple_of(index * chunk, chunk), chunk)
            for tile in range(lon_count // LANE):
                out[at, tile * LANE : (tile + 1) * LANE] = a.astype(BF)
                a, b = a * c - b * s, b * c + a * s
            return carry

        lax.fori_loop(0, block // chunk, some_rows, 0, unroll=2)

    return pl.pallas_call(
        body,
        name="wave_rows",
        grid_spec=pltpu.PrefetchScalarGridSpec(
            num_scalar_prefetch=1,
            grid=(rows // block,),
            in_specs=[],
            out_specs=pl.BlockSpec((block, lon_count), lambda i, *_: (i, 0)),
        ),
        out_shape=jax.ShapeDtypeStruct((rows, lon_count), BF),
    )(couples)


def fourier_call(place, here, waves, pieces, peers, wanted):
    parts = len(pieces)
    total_outs = len(wanted)
    rows, lons = pieces[0].shape
    columns = waves.shape[0]
    block = columns // peers

    steps = 2
    share = columns // steps

    def body(place_ref, here_ref, w_ref, *refs):
        outs = refs[parts : parts + total_outs]
        whole, total = refs[parts + total_outs :]
        step = pl.program_id(0)

        @pl.when(step == 0)
        def _():
            for d in range(parts):
                start = jnp.bitwise_xor(place_ref[0], d) * lons
                whole[:, pl.ds(pl.multiple_of(start, LANE), lons)] = refs[d][...]

        total[pl.ds(pl.multiple_of(step * share, 32), share)] = lax.dot_general(
            w_ref[...], whole[...], (((1,), (1,)), ((), ())), preferred_element_type=F32
        ).astype(BF)

        @pl.when(step == steps - 1)
        def _():
            for out, (e, first, size) in zip(outs, wanted):
                start = jnp.bitwise_xor(here_ref[0], e) * block + first
                out[...] = total[pl.ds(pl.multiple_of(start, 32), size)]

    return pl.pallas_call(
        body,
        name="fourier",
        grid_spec=pltpu.PrefetchScalarGridSpec(
            num_scalar_prefetch=2,
            grid=(steps,),
            in_specs=[pl.BlockSpec((share, parts * lons), lambda i, *_: (i, 0))]
            + [pl.BlockSpec((rows, lons), lambda i, *_: (0, 0))]
            + [pl.BlockSpec(memory_space=pltpu.VMEM)] * (parts - 1),
            out_specs=[pl.BlockSpec((size, rows), lambda i, *_: (0, 0)) for _, _, size in wanted],
            scratch_shapes=[pltpu.VMEM((rows, parts * lons), BF), pltpu.VMEM((columns, rows), BF)],
        ),
        out_shape=[jax.ShapeDtypeStruct((size, rows), BF) for _, _, size in wanted],
    )(place, here, waves, *in_vmem(pieces))


def by_slot(index, pairs, group):
    value = jnp.full(index.shape, pairs[group * GROUP], jnp.int32)
    for s in range(1, GROUP):
        value = jnp.where(index == s, pairs[group * GROUP + s], value)
    return value


def across(tiles, place):
    tiles = list(tiles)
    count = len(tiles)
    step = count // 2
    while step:
        shift = step * (LANE // count)
        upper = place // step % 2 == 1
        for d in range(count):
            if d // step % 2 == 0:
                low, high = tiles[d], tiles[d + step]
                tiles[d] = jnp.where(upper, pltpu.roll(high, shift, 1), low)
                tiles[d + step] = jnp.where(upper, high, pltpu.roll(low, LANE - shift, 1))
        step //= 2
    return tiles


def part_code(pairs, group, wave_count, half, par, lanes):
    lane = lax.broadcasted_iota(jnp.int32, (1, lanes), 1)
    slot = lane % GROUP
    r = 2 * (lane // GROUP + half) + par
    low = by_slot(slot, pairs, group)
    return 2 * slot + (r >= wave_count - low).astype(jnp.int32)


def forward_call(pairs, here, received, chunks, table, quadrature, first, groups):
    row_total, _, half_lat = table.shape
    wave_count = row_total - 1
    bands = len(received[0])
    begins = [[begin for begin, _ in parts] for parts in received]
    shares = [block for parts in received for block in in_vmem([block for _, block in parts])]
    units = chunks[-1][1]
    row_block = GROUP * 4
    fields = LANE // SUB
    rows = fields * row_block
    per = wave_count // 2 * GROUP
    where_unit = {}
    for number, (lo, hi) in enumerate(chunks):
        for unit in range(lo, hi):
            where_unit[unit] = (number, unit - lo)

    def body(pairs_ref, here_ref, *refs):
        shared = refs[: len(shares)]
        table_ref, quad_ref, out, spread = refs[len(shares) : len(shares) + 4]
        recv = refs[len(shares) + 4 :]
        group = pl.program_id(0) + first
        for number in range(len(chunks)):
            for e in range(bands):
                start = group * row_block - begins[number][e]
                mine = pl.ds(pl.multiple_of(start, row_block), row_block)
                band = jnp.bitwise_xor(here_ref[0], e)
                recv[number][band] = shared[number * bands + e][mine]
        lane = lax.broadcasted_iota(jnp.int32, (row_block, LANE), 1)
        place = lane // SUB
        turned = place * SUB + SUB - 1 - lane % SUB
        row = lax.broadcasted_iota(jnp.int32, (row_block, LANE), 0)
        low = by_slot(row // 4, pairs_ref, group)
        second = row // 2 % 2
        signs = [(1 - 2 * ((par + second * low) % 2)).astype(F32) for par in range(2)]

        def tile(band, unit):
            number, local = where_unit[unit]
            return recv[number][band, :, local * LANE : (local + 1) * LANE]

        for target in range(half_lat // LANE):
            at = slice(target * LANE, (target + 1) * LANE)
            north_tiles, south_tiles = [], []
            for d in range(fields):
                beta = fields * target + d
                band, unit = beta // units, beta % units
                north_tiles.append(tile(band, unit))
                south_tiles.append(tile(bands - 1 - band, units - 1 - unit))
            north_tiles, south_tiles = across(north_tiles, place), across(south_tiles, place)
            weight = quad_ref[0:1, at]
            for f in range(fields):
                north = north_tiles[f].astype(F32)
                south = jnp.take_along_axis(south_tiles[f].astype(F32), turned, axis=1)
                for par in range(2):
                    folded = (north + signs[par] * south) * weight
                    spread[par, f * row_block : (f + 1) * row_block, at] = folded.astype(BF)
        to = lax.broadcasted_iota(jnp.int32, (rows, rows), 0)
        source = lax.broadcasted_iota(jnp.int32, (rows, rows), 1)
        wanted = to // 2 % fields * row_block + to // (2 * fields) * 2 + to % 2
        order = (source == wanted).astype(BF)
        whole = table_ref[0:wave_count].reshape(wave_count // 2, 2, GROUP, half_lat)
        last = table_ref[wave_count]
        out[0, :, 2 * per :] = jnp.zeros((8, LANE), BF)
        for par in range(2):
            field = jnp.dot(order, spread[par], preferred_element_type=F32).astype(BF)
            matrix = whole[:, par].reshape(per, half_lat)
            product = lax.dot_general(
                field, matrix, (((1,), (1,)), ((), ())), preferred_element_type=F32
            )
            code = part_code(pairs_ref, group, wave_count, 0, par, per)
            kept = jnp.zeros((GROUP, per), F32)
            for b in range(2 * GROUP):
                kept = kept + jnp.where(code == b, product[b * 8 : (b + 1) * 8], 0.0)
            out[0, :, par * per : (par + 1) * per] = kept.astype(BF)
            if par == 0:
                ending = lax.dot_general(
                    field, last, (((1,), (1,)), ((), ())), preferred_element_type=F32
                )
                lane8 = lax.broadcasted_iota(jnp.int32, (1, GROUP), 1)
                kept = jnp.zeros((GROUP, GROUP), F32)
                for b in range(GROUP):
                    kept = kept + jnp.where(lane8 == b, ending[b * 16 + 8 : b * 16 + 16], 0.0)
                out[0, :, 2 * per : 2 * per + GROUP] = kept.astype(BF)

    return pl.pallas_call(
        body,
        name="forward",
        grid_spec=pltpu.PrefetchScalarGridSpec(
            num_scalar_prefetch=2,
            grid=(groups,),
            in_specs=[
                pl.BlockSpec(memory_space=pltpu.VMEM)
                if number % bands
                else pl.BlockSpec(block.shape, lambda g, *_: (0, 0))
                for number, block in enumerate(shares)
            ]
            + [
                pl.BlockSpec((row_total, GROUP, half_lat), lambda g, *_: (0, first + g, 0)),
                pl.BlockSpec((1, half_lat), lambda g, *_: (0, 0)),
            ],
            out_specs=pl.BlockSpec((1, 8, 2 * per + LANE), lambda g, *_: (g, 0, 0)),
            scratch_shapes=[pltpu.VMEM((2, rows, half_lat), BF)]
            + [pltpu.VMEM((bands, row_block, (hi - lo) * LANE), BF) for lo, hi in chunks],
        ),
        out_shape=jax.ShapeDtypeStruct((groups, 8, 2 * per + LANE), BF),
    )(pairs, here, *shares, table, quadrature)


def mix_matrix(operator, own):
    levels = operator.shape[0]
    n = levels * 4
    row = jnp.arange(n, dtype=jnp.int32)
    level = row // (4 * own) * own + row // 2 % own
    rest = row // (2 * own) % 2 * 2 + row % 2
    hot = (level[:, None] == jnp.arange(levels)[None, :]).astype(BF)
    spread = jnp.dot(jnp.dot(hot, operator, preferred_element_type=F32).astype(BF), hot.T,
                     preferred_element_type=F32)
    return jnp.where(rest[:, None] == rest[None, :], spread, 0.0).astype(BF)


def inverse_call(pairs, place, gathered, project, rebuild, factors, table, first, before):
    row_total, slots, half_lat = table.shape
    wave_count = row_total - 1
    lev = len(gathered)
    groups, eight, lanes = gathered[0].shape
    n = lev * eight
    per = wave_count // 2 * GROUP
    rows = 2 * GROUP * eight
    own = eight // 4

    def body(pairs_ref, place_ref, *refs):
        got = refs[:lev]
        p_ref, r_ref, f_ref, table_ref = refs[lev : lev + 4]
        out, stack, damping, x_ref = refs[-4:]
        group = pl.program_id(0) + first
        for d in range(lev):
            part = got[d][0 if d == 0 else pl.program_id(0)]
            stack[jnp.bitwise_xor(place_ref[0], d)] = part
        lane = lax.broadcasted_iota(jnp.int32, (1, lanes), 1)
        place = lane // GROUP
        half = wave_count // 2
        r = jnp.where(
            place < half, 2 * place, jnp.where(place < 2 * half, 2 * (place - half) + 1, wave_count)
        )
        low = by_slot(lane % GROUP, pairs_ref, group)
        second = r >= wave_count - low
        codes = 2 * (lane % GROUP) + second.astype(jnp.int32)
        degree = jnp.where(second, r - 1, low + r).astype(F32)
        factor = degree * (degree + 1.0) / float(wave_count * wave_count)
        levels = lev * own
        level = lax.broadcasted_iota(jnp.int32, (levels, 1), 0)
        coefficient = jnp.full((levels, 1), f_ref[0], F32)
        for q in range(1, levels):
            coefficient = jnp.where(level == q, f_ref[q], coefficient)
        damping[...] = 1.0 / (1.0 + factor * coefficient)
        values = stack[...].reshape(n, lanes)
        modes = jnp.dot(p_ref[...], values, preferred_element_type=F32)
        own_level = lax.broadcasted_iota(jnp.int32, (eight, 1), 0) // 2 % own
        damped = []
        for owner in range(lev):
            rate = damping[owner * own : owner * own + 1]
            for q in range(1, own):
                rate = jnp.where(own_level == q, damping[owner * own + q : owner * own + q + 1], rate)
            damped.append(modes[owner * eight : (owner + 1) * eight] * rate)
        damped = jnp.concatenate(damped, axis=0).astype(BF)
        x_ref[...] = jnp.dot(r_ref[...], damped, preferred_element_type=F32).astype(BF)
        whole = table_ref[0:wave_count].reshape(wave_count // 2, 2, GROUP, half_lat)
        sums = []
        for par in range(2):
            value = x_ref[:, par * per : (par + 1) * per].astype(F32)
            code = codes[:, par * per : (par + 1) * per]
            spread = jnp.concatenate(
                [jnp.where(code == b, value, 0.0) for b in range(2 * GROUP)], axis=0
            ).astype(BF)
            matrix = whole[:, par].reshape(per, half_lat)
            sums.append(jnp.dot(spread, matrix, preferred_element_type=F32))
        tail = x_ref[:, 2 * per : 2 * per + GROUP].astype(F32)
        lane8 = lax.broadcasted_iota(jnp.int32, (1, GROUP), 1)
        nothing = jnp.zeros((eight, GROUP), F32)
        spread = jnp.concatenate(
            [
                jnp.where(lane8 == b // 2, tail, 0.0) if b % 2 else nothing
                for b in range(2 * GROUP)
            ],
            axis=0,
        ).astype(BF)
        sums[0] = sums[0] + jnp.dot(spread, table_ref[wave_count], preferred_element_type=F32)
        row = lax.broadcasted_iota(jnp.int32, (rows, LANE), 0)
        low = by_slot(row // (2 * eight), pairs_ref, group)
        sign = (1 - 2 * (row // eight % 2 * low % 2)).astype(F32)
        north = sums[0] + sums[1]
        back = LANE - 1 - lax.broadcasted_iota(jnp.int32, (rows, LANE), 1)
        tiles = half_lat // LANE
        for target in range(tiles):
            source = slice((tiles - 1 - target) * LANE, (tiles - target) * LANE)
            south = sign * (sums[0][:, source] - sums[1][:, source])
            south = jnp.take_along_axis(south, back, axis=1)
            upper = north[:, target * LANE : (target + 1) * LANE]
            for b in range(2 * GROUP):
                for f in range(2 * own):
                    at = slice(b * eight + 2 * f, b * eight + 2 * f + 2)
                    place = (f // own, f % own, b // 2, b % 2)
                    out[(*place, slice(None), slice(target * LANE, (target + 1) * LANE))] = upper[at]
                    out[
                        (
                            *place,
                            slice(None),
                            slice(half_lat + target * LANE, half_lat + (target + 1) * LANE),
                        )
                    ] = south[at]

    more = () if before is None else (before,)
    return pl.pallas_call(
        body,
        name="inverse",
        grid_spec=pltpu.PrefetchScalarGridSpec(
            num_scalar_prefetch=2,
            grid=(groups,),
            in_specs=[pl.BlockSpec((1, eight, lanes), lambda g, *_: (g, 0, 0))]
            + [pl.BlockSpec(memory_space=pltpu.VMEM)] * (lev - 1)
            + [
                pl.BlockSpec((n, n), lambda g, *_: (0, 0)),
                pl.BlockSpec((eight, n), lambda g, p, q: (q[0], 0)),
                pl.BlockSpec(memory_space=pltpu.SMEM),
                pl.BlockSpec((row_total, GROUP, half_lat), lambda g, *_: (0, first + g, 0)),
            ]
            + [pl.BlockSpec(memory_space=pl.ANY)] * len(more),
            out_specs=pl.BlockSpec(
                (2, own, GROUP, 2, 2, 2 * half_lat), lambda g, *_: (0, 0, first + g, 0, 0, 0)
            ),
            scratch_shapes=[
                pltpu.VMEM((lev, eight, lanes), BF),
                pltpu.VMEM((lev * own, lanes), F32),
                pltpu.VMEM((eight, lanes), BF),
            ],
        ),
        out_shape=jax.ShapeDtypeStruct((2, own, slots, 2, 2, 2 * half_lat), F32),
        input_output_aliases={lev + 6: 0} if more else {},
    )(pairs, place, *in_vmem(gathered), project, rebuild, factors, table, *more)


def in_vmem(arrays):
    return [arrays[0]] + [pltpu.with_memory_space_constraint(x, pltpu.VMEM) for x in arrays[1:]]


def send(block, axis, bits):
    if bits == 0:
        return block
    return lax.ppermute(block, axis, [(i, i ^ bits) for i in range(lax.axis_size(axis))])


def swap(blocks, axis):
    return [send(block, axis, d) for d, block in enumerate(blocks)]


def tiled_local(u, v, t, operator, quadrature, table, couples, project, rebuild, factors):
    lev, lat = lax.axis_size("lev"), lax.axis_size("lat")
    levels, _, lons = u.shape
    own = levels // lev
    slots, row_total, _ = table.shape
    wave_count = row_total - 1
    place = lax.axis_index("lev").astype(jnp.int32)[None]
    here = lax.axis_index("lat").astype(jnp.int32)[None]
    flat = jnp.transpose(table, (1, 0, 2))
    received = []
    products = []
    for lo, hi in CHUNKS:
        products.append(products_call(place, u, v, t, operator, lev, lo, hi - lo))
    couples, products[-1] = lax.optimization_barrier((couples, products[-1]))
    waves = wave_rows_call(couples, lons * lev, wave_count)
    groups = slots // GROUP
    cut = -(-groups * CUT[0] // CUT[1])
    parts = ((0, cut), (cut, groups - cut))
    rows = 4 * GROUP
    for (lo, hi), blocks in zip(CHUNKS, products):
        came = []
        for d, block in enumerate(blocks):
            came.append(send(block, "lev", d))
        blocks = came
        if lo > 0:
            blocks, late = lax.optimization_barrier((blocks, late))
        pieces = [x.reshape((hi - lo) * LANE, lons) for x in blocks]
        ending = hi == CHUNKS[-1][1]
        near = lat // 2 if ending else lat
        wanted = [(e, 0, groups * rows) for e in range(near)]
        for first, count in parts if ending else ():
            wanted += [(e, first * rows, count * rows) for e in range(near, lat)]
        blocks = fourier_call(place, here, waves, pieces, lat, wanted)
        if lo == 0:
            blocks, late = lax.optimization_barrier(
                (blocks, (couples, quadrature, project, rebuild))
            )
            late_couples, late_quadrature, project, rebuild = late
            pairs = lax.dynamic_slice_in_dim(
                late_couples, lax.axis_index("lat") * slots, slots
            )
            to_modes = mix_matrix(project, own)
            to_levels = mix_matrix(rebuild, own)
            late = (pairs, late_quadrature[None, :], to_modes, to_levels)
        whole = [(0, send(blocks[e], "lat", e)) for e in range(near)]
        shares = []
        for number in range(len(parts) if ending else 1):
            at = slice(near + number * (lat - near), near + (number + 1) * (lat - near))
            rest = [
                (first, send(block, "lat", e))
                for block, (e, first, _) in zip(blocks[at], wanted[at])
            ]
            shares.append(whole + rest)
        received.append(shares)
    pairs, quadrature, to_modes, to_levels = late
    gathered = []
    for number, (first, count) in enumerate(parts):
        shares = [each[number if len(each) > 1 else 0] for each in received]
        block = forward_call(pairs, here, shares, CHUNKS, flat, quadrature, first, count)
        gathered.append(swap([block] * lev, "lev"))
    result = None
    for (first, _), blocks in zip(parts, gathered):
        result = inverse_call(
            pairs, place, blocks, to_modes, to_levels, factors, flat, first, result
        )
    return result


def fits(lev, lat, band, lons, levels, slots, row_total, half_lat):
    return (
        lev % 2 == 0
        and lev & (lev - 1) == 0
        and lat & (lat - 1) == 0
        and lons * lev % 8 == 0
        and 2 * (row_total - 1) * LANE < 2**8 * lons * lev
        and levels == 2 * lev
        and band == CHUNKS[-1][1] * SUB
        and lons % LANE == 0
        and slots % GROUP == 0
        and row_total % 2 == 1
        and (row_total - 1) * GROUP % (2 * LANE) == 0
        and half_lat % LANE == 0
    )


def fourier_table(position_wavenumber_couples, lon_count, wave_count):
    repeated = jnp.repeat(position_wavenumber_couples, 4)
    column = jnp.arange(repeated.shape[0], dtype=jnp.int32)
    wavenumber = jnp.where(column // 2 % 2 == 0, repeated, wave_count - 1 - repeated)
    longitude = jnp.arange(lon_count, dtype=jnp.int32)
    phase_index = longitude[:, None] * wavenumber[None, :] % lon_count
    radians = phase_index.astype(jnp.float32) * (2.0 * math.pi / lon_count)
    values = jnp.where(column % 2 == 0, jnp.cos(radians), -jnp.sin(radians)) / math.sqrt(lon_count)
    return values.astype(jnp.bfloat16)


def row_layout(low_waves, wave_count, row_index):
    row_grid = row_index[None, :]
    low_grid = low_waves[:, None]
    boundary = wave_count - low_grid
    second_part = row_grid >= boundary
    parity = jnp.where(second_part, row_grid - boundary, row_grid) % 2
    degree = jnp.where(second_part, row_grid - 1, low_grid + row_grid)
    return (second_part, parity, degree)


def row_selector(second_part, parity):
    choices_two = jnp.arange(2, dtype=jnp.int32)
    parity_hit = parity[..., None] == choices_two
    part_hit = second_part.astype(jnp.int32)[..., None] == choices_two
    return parity_hit[..., :, None] & part_hit[..., None, :]


def damping(degree, eigen_backward_factors, wave_count):
    total = degree.astype(jnp.float32)
    factor = total * (total + 1.0) / float(wave_count * wave_count)
    return 1.0 / (1.0 + factor[:, :, None] * eigen_backward_factors[None, None, :])


def forward_legendre(
    by_wave, associated_polynomial_table, quadrature_factors_north, own_pairs, wave_count
):
    field_count, layer_tally, lat_count, column_count = by_wave.shape
    half_rows = lat_count // 2
    slot_count = column_count // 4
    northern = by_wave[:, :, :half_rows].astype(jnp.float32)
    southern = by_wave[:, :, half_rows:][:, :, ::-1].astype(jnp.float32)
    folded = (
        jnp.stack([northern + southern, northern - southern]) * quadrature_factors_north[:, None]
    )
    folded = folded.astype(jnp.bfloat16).reshape(
        2, field_count, layer_tally, half_rows, slot_count, 2, 2
    )
    folded = jnp.transpose(folded, (4, 3, 0, 5, 6, 1, 2)).reshape(slot_count, half_rows, -1)
    product = jnp.einsum(
        "srl,slc->src", associated_polynomial_table, folded, preferred_element_type=jnp.float32
    )
    product = product.reshape(slot_count, wave_count + 1, 2, 2, 2, field_count, layer_tally)
    layout = row_layout(own_pairs, wave_count, jnp.arange(wave_count + 1, dtype=jnp.int32))
    chosen = row_selector(layout[0], layout[1])
    return jnp.sum(jnp.where(chosen[..., None, None, None], product, 0.0), axis=(2, 3)).astype(
        jnp.bfloat16
    )


def inverse_legendre(implicit, associated_polynomial_table, own_pairs, wave_count):
    slot_count = implicit.shape[0]
    row_total = implicit.shape[1]
    field_count = implicit.shape[3]
    layer_tally = implicit.shape[4]
    layout = row_layout(own_pairs, wave_count, jnp.arange(row_total, dtype=jnp.int32))
    chosen = row_selector(layout[0], layout[1])
    spread = jnp.where(
        chosen[..., None, None, None], implicit[:, :, None, None], jnp.zeros((), implicit.dtype)
    )
    spread = spread.reshape(slot_count, row_total, -1)
    summed = jnp.einsum(
        "srl,src->slc", associated_polynomial_table, spread, preferred_element_type=jnp.float32
    )
    summed = summed.reshape(
        slot_count, associated_polynomial_table.shape[2], 2, 2, 2, field_count, layer_tally
    )
    northern = summed[:, :, 0] + summed[:, :, 1]
    southern = (summed[:, :, 0] - summed[:, :, 1])[:, ::-1]
    latitudes = jnp.concatenate([northern, southern], axis=1)
    return jnp.transpose(latitudes, (4, 5, 0, 2, 3, 1))


def plain_local(
    zonal_velocity,
    meridional_velocity,
    air_warmth,
    pressure_integration_operator,
    quadrature_factors_north,
    associated_polynomial_table,
    position_wavenumber_couples,
    layer_projection_operator,
    eigen_reconstruction_operator,
    eigen_backward_factors,
):
    layer_tally = air_warmth.shape[0]
    gravity_potential_surface = jnp.dot(
        pressure_integration_operator,
        air_warmth.reshape(layer_tally, -1),
        preferred_element_type=jnp.float32,
    )
    gravity_potential_surface = gravity_potential_surface.reshape(air_warmth.shape)
    eastward = zonal_velocity.astype(jnp.float32)
    northward = meridional_velocity.astype(jnp.float32)
    warmth_spectrum_field = air_warmth.astype(jnp.float32)
    products = jnp.stack(
        [
            eastward * northward + gravity_potential_surface,
            (eastward + northward) * warmth_spectrum_field,
        ]
    ).astype(jnp.bfloat16)
    by_level = lax.all_to_all(products, "lev", split_axis=1, concat_axis=3, tiled=True)
    field_count = by_level.shape[0]
    own_levels = by_level.shape[1]
    band_rows = by_level.shape[2]
    lon_count = by_level.shape[3]
    slot_count = associated_polynomial_table.shape[0]
    wave_count = associated_polynomial_table.shape[1] - 1
    row_total = wave_count + 1
    transform = fourier_table(position_wavenumber_couples, lon_count, wave_count)
    harmonic_coefficients_field = jnp.dot(
        by_level.reshape(-1, lon_count), transform, preferred_element_type=jnp.float32
    )
    harmonic_coefficients_field = harmonic_coefficients_field.astype(jnp.bfloat16).reshape(
        field_count, own_levels, band_rows, -1
    )
    by_wave = lax.all_to_all(
        harmonic_coefficients_field, "lat", split_axis=3, concat_axis=2, tiled=True
    )
    own_pairs = lax.dynamic_slice_in_dim(
        position_wavenumber_couples, lax.axis_index("lat") * slot_count, slot_count
    )
    spectral = forward_legendre(
        by_wave, associated_polynomial_table, quadrature_factors_north, own_pairs, wave_count
    )
    group_size = lax.axis_size("lev")
    padded_rows = -(-row_total // group_size) * group_size
    block_rows = padded_rows // group_size
    padded = jnp.pad(spectral, ((0, 0), (0, padded_rows - row_total), (0, 0), (0, 0), (0, 0)))
    received = lax.all_to_all(padded, "lev", split_axis=1, concat_axis=4, tiled=True)
    row_index = lax.axis_index("lev") * block_rows + jnp.arange(block_rows, dtype=jnp.int32)
    degree = row_layout(own_pairs, wave_count, row_index)[2]
    level_total = received.shape[4]
    flat_rows = received.reshape(-1, level_total)
    mode_values = jnp.dot(
        flat_rows, layer_projection_operator.T, preferred_element_type=jnp.float32
    ).reshape(received.shape)
    damped = (
        mode_values * damping(degree, eigen_backward_factors, wave_count)[:, :, None, None, :]
    ).astype(jnp.bfloat16)
    result = jnp.dot(
        damped.reshape(-1, level_total),
        eigen_reconstruction_operator.T,
        preferred_element_type=jnp.float32,
    )
    result = result.reshape(received.shape).astype(jnp.bfloat16)
    implicit = lax.all_to_all(result, "lev", split_axis=4, concat_axis=1, tiled=True)[:, :row_total]
    return inverse_legendre(implicit, associated_polynomial_table, own_pairs, wave_count)


def local(*args):
    table = args[5]
    sizes = args[0].shape
    if fits(
        lax.axis_size("lev"),
        lax.axis_size("lat"),
        sizes[1],
        sizes[2],
        sizes[0],
        table.shape[0],
        table.shape[1],
        table.shape[2],
    ):
        return tiled_local(*args)
    return plain_local(*args)


def solution(mesh):
    placed = (
        P(None, "lat", "lev"),
        P(None, "lat", "lev"),
        P(None, "lat", "lev"),
        P(),
        P(),
        P("lat", None, None),
        P(),
        P(),
        P(),
        P(),
    )
    return jax.shard_map(
        local,
        mesh=mesh,
        in_specs=placed,
        out_specs=P(None, "lev", "lat", None, None, None),
        check_vma=False,
    )
```
